32 devices in a mesh: ens: 2 (over x), gy: 16 (over z, y, core).
Axes of the slice: x: 2, y: 2, z: 4, core: 2. Of those that a mesh axis runs over, the one named last changes fastest.
Arguments:
- forcing: float32 [512, 16384], P(('ens', 'gy')), parts along dimension 0, may hold values from -6 to 6
- east: float32 [256, 16384], P('gy'), may hold values from 0.5 to 2
- north: float32 [256, 16384], P('gy'), may hold values from 0.5 to 2
- storage: float32 [256, 16384], P('gy'), may hold values from 0.05 to 0.5
- coarse_inverse: float32 [64, 16, 16], replicated, as said below
- membership: int32 [4, 256], replicated, may hold values from 0 to 63, as said below
- land: int32 [4, 256], replicated, may hold values 0 or 1
Outputs:
- solution: float32 [512, 16384], P(('ens', 'gy')), parts along dimension 0
- residual: float32 [512, 16384], P(('ens', 'gy')), parts along dimension 0
The draws below stay inside these ranges and needn't reach their ends.
There are 2 independent parts, one for each index of `ens`. The reference program is written for one: setup_inputs(seed, part) draws one part's arguments, and reference() takes and returns one part's arrays. A program takes and returns all parts, laid end to end along the dimension named above; an argument that names none is the same for every part. Nothing has to cross between parts.
Inputs may be any that keep to these rules, and one draw needn't show every extreme that they name: `coarse_inverse`: each inverse is symmetric positive definite. `membership`: every basin holds one tile or more.
All inputs are finite; a program needn't handle non-finite values.
Results may differ from the reference program's by a relative error of at most 0.0003.
Values sent between devices are 32-bit elements; how exact they have to be, the bound alone decides.
A program may use at most 64 MiB of HBM per device.

```python
import math
import jax
import jax.numpy as jnp
from jax import lax

TILES_X = 256
TILE = 64
BASINS = 64
ORDER = 4
ITERS = 2
COARSE = 16
NX = 16384
NY = 256
TILE_ROWS = 4


def draw_forcing(key, part):
    return jnp.clip(jax.random.normal(key, (NY, NX), jnp.float32), -6.0, 6.0)


def draw_coarse_inverse(key, part):
    first = jax.random.fold_in(key, 11)
    second = jax.random.fold_in(key, 12)
    offdiag = jax.random.uniform(first, (BASINS, COARSE, COARSE), jnp.float32, -0.1, 0.1)
    offdiag = offdiag + jnp.swapaxes(offdiag, 1, 2)
    identity = jnp.eye(COARSE, dtype=jnp.float32)
    leading = jnp.exp(jax.random.uniform(second, (BASINS, COARSE), jnp.float32, math.log(3.5), math.log(6.0)))
    matrix = offdiag * (1.0 - identity)[None, :, :] + identity[None, :, :] * leading[:, :, None]
    cells = float(TILE_ROWS * TILES_X * TILE * TILE) / BASINS
    factor = 0.07 / math.sqrt(cells)
    return matrix * factor


def draw_membership(key, part):
    total = TILE_ROWS * TILES_X
    chosen = jax.random.permutation(jax.random.fold_in(key, 21), total)[:BASINS].astype(jnp.int32)
    seed_row = chosen // TILES_X
    seed_col = chosen % TILES_X
    rows = jnp.arange(TILE_ROWS, dtype=jnp.int32)[:, None, None]
    cols = jnp.arange(TILES_X, dtype=jnp.int32)[None, :, None]
    across = jnp.abs(cols - seed_col[None, None, :])
    across = jnp.minimum(across, TILES_X - across)
    distance = (rows - seed_row[None, None, :]) ** 2 + across ** 2
    score = distance * BASINS + jnp.arange(BASINS, dtype=jnp.int32)[None, None, :]
    return jnp.argmin(score, axis=-1).astype(jnp.int32)


def touch_ends(result, stream_key, smallest, top_value):
    index_at = [jax.random.randint(jax.random.fold_in(stream_key, axis), (), 0, length) for axis, length in enumerate(result.shape)]
    main_axis = result.shape.index(max(result.shape))
    next_to = index_at[:main_axis] + [(index_at[main_axis] + 1) % result.shape[main_axis]] + index_at[main_axis + 1:]
    return result.at[tuple(index_at)].set(smallest).at[tuple(next_to)].set(top_value)


def steps_of(stream_key, shape, shards, low, top_value):
    gain, own = 1.0, jax.random.fold_in(stream_key, 6)
    for position, shards_of in shards:
        steps = jnp.exp(jax.random.uniform(jax.random.fold_in(own, position), (shards_of,), jnp.float32, low / len(shards), top_value / len(shards)))
        gain = gain * jnp.repeat(steps, shape[position] // shards_of).reshape([-1 if axis == position else 1 for axis in range(len(shape))])
    return gain


def setup_inputs(seed: int = 0, part: int = 0) -> dict:
    keys = jax.random.split(jax.random.key(seed), 8)
    part_splits = jax.random.split(jax.random.fold_in(keys[7], part), 8)
    forcing = draw_forcing(jax.random.fold_in(jax.random.fold_in(keys[7], part), 71), part)
    east = jnp.clip(jnp.exp(math.log(2.0) - 1.3862944 * jax.random.uniform(keys[1], (NY, NX), jnp.float32) ** steps_of(keys[1], (NY, NX), ((0, 16),), -0.2, 0.2)), 0.5, 2.0)
    north = jnp.clip(jnp.exp(math.log(2.0) - 1.3862944 * jax.random.uniform(keys[2], (NY, NX), jnp.float32) ** steps_of(keys[2], (NY, NX), ((0, 16),), -0.2, 0.2)), 0.5, 2.0)
    storage = jnp.clip(jnp.exp(math.log(0.5) - 2.3025851 * jax.random.uniform(keys[3], (NY, NX), jnp.float32) ** steps_of(keys[3], (NY, NX), ((0, 16),), -0.2, 0.2)), 0.05, 0.5)
    coarse_inverse = draw_coarse_inverse(jax.random.fold_in(keys[7], 71), part)
    membership = draw_membership(jax.random.fold_in(keys[7], 71), part)
    land = touch_ends((jax.random.randint(keys[6], (TILE_ROWS, TILES_X), 0, 4) < 1).astype(jnp.int32), jax.random.fold_in(keys[6], 1), 0, 1)
    return dict(forcing=forcing, east=east, north=north, storage=storage, coarse_inverse=coarse_inverse, membership=membership, land=land)


HIGHEST = lax.Precision.HIGHEST


def mode_table():
    degree = jnp.arange(ORDER).astype(jnp.float32)
    local = jnp.arange(TILE).astype(jnp.float32)
    return jnp.cos(jnp.pi * degree[:, None] * (local[None, :] + 0.5) / TILE)


def reference(forcing, east, north, storage, coarse_inverse, membership, land):
    tile_rows, tiles_x = membership.shape
    modes = mode_table()
    wet = jnp.repeat(jnp.repeat(1.0 - land.astype(jnp.float32), TILE, axis=0), TILE, axis=1)
    above = jnp.concatenate([wet[1:], jnp.zeros_like(wet[:1])], axis=0)
    east_face = east * wet * jnp.roll(wet, -1, axis=1)
    north_face = north * wet * above
    south_face = jnp.concatenate([jnp.zeros_like(north_face[:1]), north_face[:-1]], axis=0)
    west_face = jnp.roll(east_face, 1, axis=1)
    center = (1.0 - wet) + wet * storage + east_face + west_face + north_face + south_face
    jacobi = 1.0 / center
    owned = (membership[:, :, None] == jnp.arange(BASINS)[None, None, :]).astype(jnp.float32)

    def operate(field):
        north_v = jnp.concatenate([field[1:], jnp.zeros_like(field[:1])], axis=0)
        south_v = jnp.concatenate([jnp.zeros_like(field[:1]), field[:-1]], axis=0)
        return (center * field - east_face * jnp.roll(field, -1, axis=1) - west_face * jnp.roll(field, 1, axis=1)
                - north_face * north_v - south_face * south_v)

    def precondition(field):
        blocks = (wet * field).reshape(tile_rows, TILE, tiles_x, TILE)
        lifted = jnp.einsum("aibk,pi->apbk", blocks, modes, precision=HIGHEST)
        per_tile = jnp.einsum("apbk,qk->abpq", lifted, modes, precision=HIGHEST).reshape(tile_rows, tiles_x, COARSE)
        sums = jnp.einsum("abn,abc->nc", owned, per_tile, precision=HIGHEST)
        coef = jnp.einsum("nij,nj->ni", coarse_inverse, sums, precision=HIGHEST)
        tile_coef = jnp.einsum("abn,nc->abc", owned, coef, precision=HIGHEST).reshape(tile_rows, tiles_x, ORDER, ORDER)
        spread = jnp.einsum("abpq,qk->apbk", tile_coef, modes, precision=HIGHEST)
        back = jnp.einsum("apbk,pi->aibk", spread, modes, precision=HIGHEST).reshape(field.shape)
        return jacobi * field + wet * back

    solution = jnp.zeros_like(forcing)
    residual = forcing
    smoothed = precondition(residual)
    direction = smoothed
    energy = jnp.sum(residual * smoothed)
    for step in range(ITERS):
        image = operate(direction)
        alpha = energy / jnp.sum(direction * image)
        solution = solution + alpha * direction
        residual = residual - alpha * image
        smoothed = precondition(residual)
        energy_next = jnp.sum(residual * smoothed)
        direction = smoothed + (energy_next / energy) * direction
        energy = energy_next
    return solution, residual
```

```python
import functools

import jax
import jax.numpy as jnp
import numpy as np
from jax import lax
from jax.experimental import pallas as pl
from jax.experimental.pallas import tpu as pltpu
from jax.sharding import PartitionSpec as P

TILE = 64
ORDER = 4
LANES = 128
BLOCKS = 8
HIGHEST = lax.Precision.HIGHEST
MESH = pl.DeviceIdType.MESH


def tables():
    degree = np.arange(ORDER, dtype=np.float64)
    local = np.arange(TILE, dtype=np.float64)
    modes = np.cos(np.pi * degree[:, None] * (local[None, :] + 0.5) / TILE).astype(np.float32)
    by_row = np.repeat(modes[:, :, None], LANES, axis=2)
    kron = np.zeros((ORDER * ORDER, ORDER * LANES), np.float32)
    for p in range(ORDER):
        for q in range(ORDER):
            kron[p * ORDER + q, p * LANES : (p + 1) * LANES] = np.tile(modes[q], LANES // TILE)
    return by_row, kron


def dot(a, b, contract=((1,), (0,))):
    return lax.dot_general(
        a, b, (contract, ((), ())), precision=HIGHEST, preferred_element_type=jnp.float32
    )


def kernel(
    n,
    forcing_hbm, east_hbm, north_hbm, storage_hbm, inverse_hbm,
    membership_ref, land_ref, by_row_ref, kron_ref,
    sol_ref, res_ref,
    f_ref, east_ref, north_ref, storage_ref, inv_ref,
    e_ref, w_ref, s_ref, c_ref, j_ref, sm_ref, q_ref, z0_ref, z1_ref, im0_ref, im1_ref,
    mask_ref, own_ref, spread_ref, edge_ref, lift_ref, ct_ref,
    nlo_ref, smlo_ref, smhi_ref, qlo_ref, qhi_ref,
    send_ref, recv_ref,
    in_sem, row_send_sem, row_recv_sem, all_send_sem, all_recv_sem,
):
    rows, width = f_ref.shape
    basins = inv_ref.shape[0]
    coarse = inv_ref.shape[1]
    blocks = width // LANES
    half = LANES // 2
    span = BLOCKS * LANES
    chunks = width // span
    tile_rows = membership_ref.shape[0]
    me = lax.axis_index("gy")
    start = me * rows
    has_up = me < n - 1
    has_down = me > 0

    def load(src, dst, k):
        return pltpu.make_async_copy(src, dst, in_sem.at[k])

    loads = [
        load(forcing_hbm, f_ref, 0),
        load(north_hbm, north_ref, 1),
        load(east_hbm, east_ref.at[:, pl.ds(LANES, width)], 2),
        load(east_hbm.at[:, pl.ds(width - LANES, LANES)], east_ref.at[:, pl.ds(0, LANES)], 3),
        load(storage_hbm, storage_ref, 4),
        load(inverse_hbm, inv_ref, 5),
    ]
    for copy in loads:
        copy.start()

    barrier = pltpu.get_barrier_semaphore()

    def greet(k, carry):
        pl.semaphore_signal(
            barrier, inc=1, device_id={"gy": lax.rem(me + k, n)}, device_id_type=MESH
        )
        return carry

    lax.fori_loop(1, n, greet, 0)

    own_row = start // TILE
    up_row = jnp.minimum((start + rows) // TILE, tile_rows - 1)
    down_row = jnp.maximum(start - 1, 0) // TILE
    local_own = pl.multiple_of(lax.rem(start, TILE), rows)
    local_up = lax.rem(start + rows, TILE)
    local_down = lax.rem(start + TILE - 1, TILE)

    tiles = membership_ref.shape[1]
    tile_id = lax.broadcasted_iota(jnp.int32, (blocks, tiles), 1)
    block_id = lax.broadcasted_iota(jnp.int32, (blocks, tiles), 0)
    even = tile_id == 2 * block_id
    odd = tile_id == 2 * block_id + 1
    lane = lax.broadcasted_iota(jnp.int32, (blocks, LANES), 1)
    left = lane < half
    basin_of_lane = jnp.where(left, lane, lane - half)

    def columns(table, row):
        line = table[pl.ds(row, 1), :].astype(jnp.float32)
        first = jnp.sum(jnp.where(even, line, 0.0), axis=1, keepdims=True)
        second = jnp.sum(jnp.where(odd, line, 0.0), axis=1, keepdims=True)
        return (
            jnp.broadcast_to(first, (blocks, LANES)),
            jnp.broadcast_to(second, (blocks, LANES)),
        )

    def owned(row, wet0, wet1):
        first, second = columns(membership_ref, row)
        which = jnp.where(left, first, second)
        hit = which == basin_of_lane.astype(jnp.float32)
        return jnp.where(hit, jnp.where(left, wet0, wet1), 0.0)

    def wets(row):
        first, second = columns(land_ref, row)
        return 1.0 - first, 1.0 - second

    wet0, wet1 = wets(own_row)
    wet = jnp.where(left, wet0, wet1)
    east_wet = jnp.where(
        lane == half - 1, wet1, jnp.where(lane == LANES - 1, pltpu.roll(wet0, blocks - 1, 0), wet)
    )
    west_wet = jnp.where(lane == 0, pltpu.roll(wet1, 1, 0), jnp.where(lane == half, wet0, wet))
    up0, up1 = wets(up_row)
    down0, down1 = wets(down_row)
    mask_ref[0] = wet
    mask_ref[1] = wet * east_wet
    mask_ref[2] = wet * west_wet
    mask_ref[3] = jnp.where(has_up, wet * jnp.where(left, up0, up1), 0.0)
    mask_ref[4] = jnp.where(has_down, wet * jnp.where(left, down0, down1), 0.0)
    own_ref[0] = owned(own_row, wet0, wet1)
    own_ref[1] = own_ref[0].T
    own_ref[2] = owned(down_row, down0, down1)
    own_ref[3] = owned(up_row, up0, up1)

    row_modes = [by_row_ref[p, pl.ds(local_own, rows), :] for p in range(ORDER)]
    up_modes = [by_row_ref[p, pl.ds(local_up, 1), :] for p in range(ORDER)]
    down_modes = [by_row_ref[p, pl.ds(local_down, 1), :] for p in range(ORDER)]

    def wide(v):
        return jnp.concatenate([v] * BLOCKS, axis=1)

    def group(c):
        return pl.ds(pl.multiple_of(c * BLOCKS, BLOCKS), BLOCKS)

    def line_of(ref, c, lane0=0):
        block = ref[group(c), lane0 : lane0 + LANES]
        return jnp.concatenate([block[t : t + 1, :] for t in range(BLOCKS)], axis=1)

    def cols(c, offset=0, extra=0):
        return pl.ds(pl.multiple_of(c * span + offset, LANES), span + extra)

    row_id = lax.broadcasted_iota(jnp.int32, (rows, span), 0)

    sub = lax.broadcasted_iota(jnp.int32, (8, LANES), 0)

    def sum_rows(parts):
        for bit in (4, 2, 1):
            lower = lax.rem(sub // bit, 2) == 0
            merged = []
            for t in range(bit):
                a, b = parts[t], parts[t + bit]
                other = jnp.where(lower, b, a)
                turned = pltpu.roll(other, 8 - bit, 0)
                if bit != 4:
                    turned = jnp.where(lower, turned, pltpu.roll(other, bit, 0))
                merged.append(jnp.where(lower, a, b) + turned)
            parts = merged
        return parts[0]

    def lift(c, field):
        for p in range(ORDER):
            parts = []
            for t in range(BLOCKS):
                block = field[:, t * LANES : (t + 1) * LANES] * row_modes[p]
                parts.append(functools.reduce(
                    lambda a, b: a + b, [block[i : i + 8] for i in range(0, rows, 8)]
                ))
            lift_ref[group(c), p * LANES : (p + 1) * LANES] = sum_rows(parts)

    half_row = lax.broadcasted_iota(jnp.int32, (LANES, ORDER * LANES), 0) < half
    half_col = (
        lax.rem(lax.broadcasted_iota(jnp.int32, (LANES, ORDER * LANES), 1), LANES) < half
    )
    same_half = half_row == half_col
    left8 = lax.broadcasted_iota(jnp.int32, (coarse // 2, LANES), 1) < half

    def packed_moments():
        sums = dot(own_ref[1], lift_ref[...])
        sums = jnp.where(same_half, sums, 0.0)
        g = dot(kron_ref[...], sums, ((1,), (1,)))
        g = g + pltpu.roll(g, half, 1)
        return jnp.where(left8, g[: coarse // 2], g[coarse // 2 :])

    def unpacked(packed):
        turned = pltpu.roll(packed, half, 1)
        return jnp.concatenate(
            [jnp.where(left8, packed, turned), jnp.where(left8, turned, packed)], axis=0
        )

    def remote(src, dst, send_sem, recv_sem, peer):
        return pltpu.make_async_remote_copy(
            src_ref=src, dst_ref=dst, send_sem=send_sem, recv_sem=recv_sem,
            device_id={"gy": peer}, device_id_type=MESH,
        )

    part = (8, 16, 8)
    first_row = (0, 0, 8)

    def exchange(k, peer_step):
        peer = lax.rem(me + peer_step, n)
        window = pl.ds(first_row[k], part[k])
        return remote(
            send_ref.at[k, window], recv_ref.at[k, me, window],
            all_send_sem.at[k, peer_step], all_recv_sem.at[k, me], peer,
        )

    def send_all(k):
        def go(step, carry):
            exchange(k, step).start()
            return carry

        lax.fori_loop(1, n, go, 0, unroll=n <= 16)
        recv_ref[k, me] = send_ref[k]

    def wait_all(k):
        window = pl.ds(first_row[k], part[k])

        def go(step, carry):
            peer = lax.rem(me + step, n)
            remote(
                send_ref.at[k, window], recv_ref.at[k, peer, window],
                all_send_sem.at[k, step], all_recv_sem.at[k, peer], peer,
            ).wait_recv()
            return carry

        lax.fori_loop(1, n, go, 0, unroll=n <= 16)
        parts = [recv_ref[k, i, first_row[k] : first_row[k] + part[k], :] for i in range(n)]
        while len(parts) > 1:
            parts = [parts[i] + parts[i + 1] for i in range(0, len(parts) - 1, 2)] + (
                [parts[-1]] if len(parts) % 2 else []
            )
        return parts[0]

    def row_up(src, dst, k):
        return remote(src, dst, row_send_sem.at[k], row_recv_sem.at[k], me + 1)

    def row_down(src, dst, k):
        return remote(src, dst, row_send_sem.at[k], row_recv_sem.at[k], me - 1)

    last = pl.ds(rows - 1, 1)
    first = pl.ds(0, 1)
    north_up = row_up(north_ref.at[last], nlo_ref, 0)
    sm_up = row_up(sm_ref.at[last], smlo_ref, 1)
    sm_down = row_down(sm_ref.at[first], smhi_ref, 2)
    q_up = row_up(q_ref.at[last], qlo_ref, 3)
    q_down = row_down(q_ref.at[first], qhi_ref, 4)

    @pl.when(jnp.logical_not(has_down))
    def _():
        for ref in (nlo_ref, smlo_ref, qlo_ref):
            ref[...] = jnp.zeros_like(ref)

    @pl.when(jnp.logical_not(has_up))
    def _():
        for ref in (smhi_ref, qhi_ref):
            ref[...] = jnp.zeros_like(ref)

    loads[0].wait()

    def first_moments(c, carry):
        lift(c, f_ref[:, cols(c)])
        return carry

    lax.fori_loop(0, chunks, first_moments, 0)
    send_ref[0, 0:8] = packed_moments()
    send_ref[0, 8:16] = jnp.zeros((8, LANES), jnp.float32)
    loads[1].wait()
    pl.semaphore_wait(barrier, n - 1)
    send_all(0)

    @pl.when(has_up)
    def _():
        north_up.start()

    loads[2].wait()
    loads[3].wait()
    loads[4].wait()
    loads[5].wait()

    identity = (
        lax.broadcasted_iota(jnp.int32, (coarse, coarse), 0)
        == lax.broadcasted_iota(jnp.int32, (coarse, coarse), 1)
    ).astype(jnp.float32)
    for k in range(coarse):
        block = inv_ref[:, k, :]
        ct_ref[k] = dot(identity, jnp.concatenate([block, block], axis=0), ((1,), (1,)))

    @pl.when(has_down)
    def _():
        north_up.wait_recv()

    def coefficients(c, energy):
        at = cols(c)
        here = line_of(mask_ref.at[0], c)
        raw = east_ref[:, pl.ds(pl.multiple_of(c * span, LANES), span + LANES)]
        e = raw[:, LANES:] * line_of(mask_ref.at[1], c)
        w = pltpu.roll(raw, 1, 1)[:, LANES:] * line_of(mask_ref.at[2], c)
        nf = north_ref[:, at] * jnp.where(row_id == rows - 1, line_of(mask_ref.at[3], c), here)
        sf = jnp.where(
            row_id == 0, nlo_ref[:, at] * line_of(mask_ref.at[4], c), pltpu.roll(nf, 1, 0)
        )
        center = (1.0 - here) + here * storage_ref[:, at] + e + w + nf + sf
        jacobi = 1.0 / center
        f = f_ref[:, at]
        smoothed = jacobi * f
        e_ref[:, at] = e
        w_ref[:, at] = w
        s_ref[:, at] = sf
        c_ref[:, at] = center
        j_ref[:, at] = jacobi
        sm_ref[:, at] = smoothed
        return energy + f * smoothed

    zero = jnp.zeros((rows, span), jnp.float32)

    energy_part = lax.fori_loop(0, chunks, coefficients, zero)

    @pl.when(has_up)
    def _():
        sm_up.start()

    @pl.when(has_down)
    def _():
        sm_down.start()

    def lane_sums(v):
        v = jnp.sum(v, axis=0, keepdims=True)
        return functools.reduce(
            lambda a, b: a + b, [v[:, t * LANES : (t + 1) * LANES] for t in range(BLOCKS)]
        )

    def dots_rows(a, b):
        r = lax.broadcasted_iota(jnp.int32, (8, LANES), 0)
        return jnp.where(r == 0, lane_sums(a), jnp.where(r == 1, lane_sums(b), 0.0))

    def total(block, row):
        return jnp.sum(block[row : row + 1, :], axis=1, keepdims=True)

    def expand(g):
        c = ct_ref[0] * g[0:1, :]
        for k in range(1, coarse):
            c = c + ct_ref[k] * g[k : k + 1, :]
        gc = jnp.sum(jnp.sum(g * c, axis=0, keepdims=True)[:, :half], axis=1, keepdims=True)
        d = dot(c.T, kron_ref[...])
        d = jnp.where(same_half, d, 0.0)
        spread_ref[...] = dot(own_ref[0], d)

        def edge(modes):
            return functools.reduce(
                lambda a, b: a + b,
                [modes[p] * d[:, p * LANES : (p + 1) * LANES] for p in range(ORDER)],
            )

        edge_ref[0] = dot(own_ref[2], edge(down_modes))
        edge_ref[1] = dot(own_ref[3], edge(up_modes))
        return gc

    def spread(c):
        return functools.reduce(
            lambda a, b: a + b,
            [wide(row_modes[p]) * line_of(spread_ref, c, p * LANES) for p in range(ORDER)],
        )

    def wrap(ref):
        ref[:, 0:LANES] = ref[:, width : width + LANES]
        ref[:, width + LANES : width + 2 * LANES] = ref[:, LANES : 2 * LANES]

    def operate(z_ref, c, low, high, nf):
        at = cols(c)
        window = z_ref[:, cols(c, 0, 2 * LANES)]
        size = span + 2 * LANES
        v = window[:, LANES : LANES + span]
        east_v = pltpu.roll(window, size - 1, 1)[:, LANES : LANES + span]
        west_v = pltpu.roll(window, 1, 1)[:, LANES : LANES + span]
        north_v = jnp.where(row_id == rows - 1, high, pltpu.roll(v, rows - 1, 0))
        south_v = jnp.where(row_id == 0, low, pltpu.roll(v, 1, 0))
        image = (
            c_ref[:, at] * v - e_ref[:, at] * east_v - w_ref[:, at] * west_v
            - nf * north_v - s_ref[:, at] * south_v
        )
        return v, image

    g = unpacked(wait_all(0))
    coarse_energy = expand(g)

    def north_of(c):
        return north_ref[:, cols(c)] * jnp.where(
            row_id == rows - 1, line_of(mask_ref.at[3], c), line_of(mask_ref.at[0], c)
        )

    def precondition0(c, carry):
        z0_ref[:, cols(c, LANES)] = sm_ref[:, cols(c)] + spread(c)
        return carry

    lax.fori_loop(0, chunks, precondition0, 0)
    wrap(z0_ref)

    @pl.when(has_down)
    def _():
        sm_up.wait_recv()

    @pl.when(has_up)
    def _():
        sm_down.wait_recv()

    def image0(c, along):
        at = cols(c)
        low = smlo_ref[:, at] + line_of(edge_ref.at[0], c)
        high = smhi_ref[:, at] + line_of(edge_ref.at[1], c)
        v, image = operate(z0_ref, c, low, high, north_of(c))
        im0_ref[:, at] = image
        q_ref[:, at] = j_ref[:, at] * image
        lift(c, image)
        return along + v * image

    along_part = lax.fori_loop(0, chunks, image0, zero)

    @pl.when(has_up)
    def _():
        q_up.start()

    @pl.when(has_down)
    def _():
        q_down.start()

    send_ref[1, 0:8] = packed_moments()
    send_ref[1, 8:16] = dots_rows(energy_part, along_part)
    send_all(1)
    sums = wait_all(1)
    energy = total(sums[8:16], 0) + coarse_energy
    alpha = energy / total(sums[8:16], 1)
    g = g - alpha * unpacked(sums[0:8])
    coarse_energy = expand(g)

    def precondition1(c, acc):
        at = cols(c)
        smoothed = sm_ref[:, at] - alpha * q_ref[:, at]
        residual = f_ref[:, at] - alpha * im0_ref[:, at]
        f_ref[:, at] = residual
        z1_ref[:, cols(c, LANES)] = smoothed + spread(c)
        return acc + residual * smoothed

    energy_part = lax.fori_loop(0, chunks, precondition1, zero)
    wrap(z1_ref)

    @pl.when(has_down)
    def _():
        q_up.wait_recv()

    @pl.when(has_up)
    def _():
        q_down.wait_recv()

    def image1(c, along):
        at = cols(c)
        low = smlo_ref[:, at] - alpha * qlo_ref[:, at] + line_of(edge_ref.at[0], c)
        high = smhi_ref[:, at] - alpha * qhi_ref[:, at] + line_of(edge_ref.at[1], c)
        v, image = operate(z1_ref, c, low, high, north_of(c))
        im1_ref[:, at] = image
        return along + v * image

    along_part = lax.fori_loop(0, chunks, image1, zero)
    send_ref[2, 0:8] = jnp.zeros((8, LANES), jnp.float32)
    send_ref[2, 8:16] = dots_rows(energy_part, along_part)
    send_all(2)
    sums = wait_all(2)
    energy_next = total(sums, 0) + coarse_energy
    beta = energy_next / energy
    alpha_next = energy_next / (total(sums, 1) - beta * energy_next / alpha)

    def finish(c, carry):
        at = cols(c)
        z0 = z0_ref[:, cols(c, LANES)]
        sol_ref[:, at] = alpha * z0 + alpha_next * (z1_ref[:, cols(c, LANES)] + beta * z0)
        res_ref[:, at] = f_ref[:, at] - alpha_next * (im1_ref[:, at] + beta * im0_ref[:, at])
        return carry

    lax.fori_loop(0, chunks, finish, 0)

    @pl.when(has_up)
    def _():
        north_up.wait_send()
        sm_up.wait_send()
        q_up.wait_send()

    @pl.when(has_down)
    def _():
        sm_down.wait_send()
        q_down.wait_send()

    for k in range(3):
        def drain(step, carry):
            exchange(k, step).wait_send()
            return carry

        lax.fori_loop(1, n, drain, 0, unroll=n <= 16)


def body(forcing, east, north, storage, coarse_inverse, membership, land):
    n = lax.axis_size("gy")
    rows, width = forcing.shape
    basins, coarse, _ = coarse_inverse.shape
    by_row, kron = tables()
    field = pltpu.VMEM((rows, width), jnp.float32)
    padded = pltpu.VMEM((rows, width + 2 * LANES), jnp.float32)
    line = pltpu.VMEM((1, width), jnp.float32)
    blocks = width // LANES
    hbm = pl.BlockSpec(memory_space=pl.ANY)
    vmem = pl.BlockSpec(memory_space=pltpu.VMEM)
    return pl.pallas_call(
        functools.partial(kernel, n),
        out_shape=[jax.ShapeDtypeStruct((rows, width), jnp.float32)] * 2,
        in_specs=[hbm] * 5 + [vmem] * 4,
        out_specs=[vmem] * 2,
        scratch_shapes=[
            field, padded, field, field, pltpu.VMEM((basins, coarse, coarse), jnp.float32),
            field, field, field, field, field, field, field, padded, padded, field, field,
            pltpu.VMEM((5, blocks, LANES), jnp.float32),
            pltpu.VMEM((4, blocks, LANES), jnp.float32),
            pltpu.VMEM((blocks, ORDER * LANES), jnp.float32),
            pltpu.VMEM((2, blocks, LANES), jnp.float32),
            pltpu.VMEM((blocks, ORDER * LANES), jnp.float32),
            pltpu.VMEM((coarse, coarse, LANES), jnp.float32),
            line, line, line, line, line,
            pltpu.VMEM((3, 16, LANES), jnp.float32),
            pltpu.VMEM((3, n, 16, LANES), jnp.float32),
            pltpu.SemaphoreType.DMA((6,)),
            pltpu.SemaphoreType.DMA((5,)),
            pltpu.SemaphoreType.DMA((5,)),
            pltpu.SemaphoreType.DMA((3, n)),
            pltpu.SemaphoreType.DMA((3, n)),
        ],
        compiler_params=pltpu.CompilerParams(
            collective_id=0, has_side_effects=True, vmem_limit_bytes=48 * 1024 * 1024
        ),
        name="solve",
    )(forcing, east, north, storage, coarse_inverse, membership, land, jnp.asarray(by_row), jnp.asarray(kron))


def solution(mesh):
    return jax.shard_map(
        body,
        mesh=mesh,
        in_specs=(
            P(("ens", "gy"), None),
            P("gy", None),
            P("gy", None),
            P("gy", None),
            P(),
            P(),
            P(),
        ),
        out_specs=(P(("ens", "gy"), None), P(("ens", "gy"), None)),
        check_vma=False,
    )
```

```python
import functools

import jax
import jax.numpy as jnp
import numpy as np
from jax import lax
from jax.experimental import pallas as pl
from jax.experimental.pallas import tpu as pltpu
from jax.sharding import PartitionSpec as P

TILE = 64
ORDER = 4
LANES = 128
BLOCKS = 8
VMEM = 67043328
SPARE = 400 * 1024
HIGHEST = lax.Precision.HIGHEST
MESH = pl.DeviceIdType.MESH


def tables():
    degree = np.arange(ORDER, dtype=np.float64)
    local = np.arange(TILE, dtype=np.float64)
    modes = np.cos(np.pi * degree[:, None] * (local[None, :] + 0.5) / TILE).astype(np.float32)
    by_row = np.repeat(modes[:, :, None], LANES, axis=2)
    kron = np.zeros((ORDER * ORDER, ORDER * LANES), np.float32)
    for p in range(ORDER):
        for q in range(ORDER):
            kron[p * ORDER + q, p * LANES : (p + 1) * LANES] = np.tile(modes[q], LANES // TILE)
    return by_row, kron


def dot(a, b, contract=((1,), (0,))):
    return lax.dot_general(
        a, b, (contract, ((), ())), precision=HIGHEST, preferred_element_type=jnp.float32
    )


def kernel(
    n,
    forcing_hbm, east_hbm, north_hbm, storage_hbm, inv_ref,
    membership_ref, land_ref, by_row_ref, kron_ref,
    sol_ref, res_ref,
    f_ref, east_ref, north_ref, storage_ref,
    e_ref, w_ref, s_ref, c_ref, j_ref, sm_ref, q_ref, z0_ref, z1_ref, im0_ref, im1_ref,
    mask_ref, own_ref, spread_ref, edge_ref, lift_ref, ct_ref,
    nlo_ref, smlo_ref, smhi_ref, qlo_ref, qhi_ref,
    send_ref, recv_ref,
    in_sem, row_send_sem, row_recv_sem, all_send_sem, all_recv_sem,
):
    rows, width = f_ref.shape
    coarse = inv_ref.shape[0]
    blocks = width // LANES
    half = LANES // 2
    span = BLOCKS * LANES
    chunks = width // span
    tile_rows = membership_ref.shape[0]
    me = lax.axis_index("gy")
    start = me * rows
    has_up = me < n - 1
    has_down = me > 0

    def load(src, dst, k):
        return pltpu.make_async_copy(src, dst, in_sem.at[k])

    loads = [
        load(forcing_hbm, f_ref, 0),
        load(north_hbm, north_ref, 1),
        load(east_hbm, east_ref.at[:, pl.ds(LANES, width)], 2),
        load(east_hbm.at[:, pl.ds(width - LANES, LANES)], east_ref.at[:, pl.ds(0, LANES)], 3),
        load(storage_hbm, storage_ref, 4),
    ]
    for copy in loads:
        copy.start()

    barrier = pltpu.get_barrier_semaphore()

    def greet(k, carry):
        pl.semaphore_signal(
            barrier, inc=1, device_id={"gy": lax.rem(me + k, n)}, device_id_type=MESH
        )
        return carry

    lax.fori_loop(1, n, greet, 0)

    own_row = start // TILE
    up_row = jnp.minimum((start + rows) // TILE, tile_rows - 1)
    down_row = jnp.maximum(start - 1, 0) // TILE
    local_own = pl.multiple_of(lax.rem(start, TILE), rows)
    local_up = lax.rem(start + rows, TILE)
    local_down = lax.rem(start + TILE - 1, TILE)

    tiles = membership_ref.shape[1]
    tile_id = lax.broadcasted_iota(jnp.int32, (blocks, tiles), 1)
    block_id = lax.broadcasted_iota(jnp.int32, (blocks, tiles), 0)
    even = tile_id == 2 * block_id
    odd = tile_id == 2 * block_id + 1
    lane = lax.broadcasted_iota(jnp.int32, (blocks, LANES), 1)
    left = lane < half
    basin_of_lane = jnp.where(left, lane, lane - half)

    def columns(table, row):
        line = table[pl.ds(row, 1), :].astype(jnp.float32)
        first = jnp.sum(jnp.where(even, line, 0.0), axis=1, keepdims=True)
        second = jnp.sum(jnp.where(odd, line, 0.0), axis=1, keepdims=True)
        return (
            jnp.broadcast_to(first, (blocks, LANES)),
            jnp.broadcast_to(second, (blocks, LANES)),
        )

    def owned(row, wet0, wet1):
        first, second = columns(membership_ref, row)
        which = jnp.where(left, first, second)
        hit = which == basin_of_lane.astype(jnp.float32)
        return jnp.where(hit, jnp.where(left, wet0, wet1), 0.0)

    def wets(row):
        first, second = columns(land_ref, row)
        return 1.0 - first, 1.0 - second

    wet0, wet1 = wets(own_row)
    wet = jnp.where(left, wet0, wet1)
    east_wet = jnp.where(
        lane == half - 1, wet1, jnp.where(lane == LANES - 1, pltpu.roll(wet0, blocks - 1, 0), wet)
    )
    west_wet = jnp.where(lane == 0, pltpu.roll(wet1, 1, 0), jnp.where(lane == half, wet0, wet))
    up0, up1 = wets(up_row)
    down0, down1 = wets(down_row)
    mask_ref[0] = wet
    mask_ref[1] = wet * east_wet
    mask_ref[2] = wet * west_wet
    mask_ref[3] = jnp.where(has_up, wet * jnp.where(left, up0, up1), 0.0)
    mask_ref[4] = jnp.where(has_down, wet * jnp.where(left, down0, down1), 0.0)
    own_ref[0] = owned(own_row, wet0, wet1)
    own_ref[1] = own_ref[0].T
    own_ref[2] = owned(down_row, down0, down1)
    own_ref[3] = owned(up_row, up0, up1)

    row_modes = [by_row_ref[p, pl.ds(local_own, rows), :] for p in range(ORDER)]
    up_modes = [by_row_ref[p, pl.ds(local_up, 1), :] for p in range(ORDER)]
    down_modes = [by_row_ref[p, pl.ds(local_down, 1), :] for p in range(ORDER)]

    def wide(v):
        return jnp.concatenate([v] * BLOCKS, axis=1)

    def group(c):
        return pl.ds(pl.multiple_of(c * BLOCKS, BLOCKS), BLOCKS)

    def line_of(ref, c, lane0=0):
        block = ref[group(c), lane0 : lane0 + LANES]
        return jnp.concatenate([block[t : t + 1, :] for t in range(BLOCKS)], axis=1)

    def cols(c, offset=0, extra=0):
        return pl.ds(pl.multiple_of(c * span + offset, LANES), span + extra)

    row_id = lax.broadcasted_iota(jnp.int32, (rows, span), 0)

    sub = lax.broadcasted_iota(jnp.int32, (8, LANES), 0)

    def sum_rows(parts):
        for bit in (4, 2, 1):
            lower = lax.rem(sub // bit, 2) == 0
            merged = []
            for t in range(bit):
                a, b = parts[t], parts[t + bit]
                other = jnp.where(lower, b, a)
                turned = pltpu.roll(other, 8 - bit, 0)
                if bit != 4:
                    turned = jnp.where(lower, turned, pltpu.roll(other, bit, 0))
                merged.append(jnp.where(lower, a, b) + turned)
            parts = merged
        return parts[0]

    def lift(c, field):
        for p in range(ORDER):
            parts = []
            for t in range(BLOCKS):
                block = field[:, t * LANES : (t + 1) * LANES] * row_modes[p]
                parts.append(functools.reduce(
                    lambda a, b: a + b, [block[i : i + 8] for i in range(0, rows, 8)]
                ))
            lift_ref[group(c), p * LANES : (p + 1) * LANES] = sum_rows(parts)

    half_row = lax.broadcasted_iota(jnp.int32, (LANES, ORDER * LANES), 0) < half
    half_col = (
        lax.rem(lax.broadcasted_iota(jnp.int32, (LANES, ORDER * LANES), 1), LANES) < half
    )
    same_half = half_row == half_col
    left8 = lax.broadcasted_iota(jnp.int32, (coarse // 2, LANES), 1) < half

    def packed_moments():
        sums = dot(own_ref[1], lift_ref[...])
        sums = jnp.where(same_half, sums, 0.0)
        g = dot(kron_ref[...], sums, ((1,), (1,)))
        g = g + pltpu.roll(g, half, 1)
        return jnp.where(left8, g[: coarse // 2], g[coarse // 2 :])

    def unpacked(packed):
        turned = pltpu.roll(packed, half, 1)
        return jnp.concatenate(
            [jnp.where(left8, packed, turned), jnp.where(left8, turned, packed)], axis=0
        )

    def remote(src, dst, send_sem, recv_sem, peer):
        return pltpu.make_async_remote_copy(
            src_ref=src, dst_ref=dst, send_sem=send_sem, recv_sem=recv_sem,
            device_id={"gy": peer}, device_id_type=MESH,
        )

    part = (8, 16, 8)
    first_row = (0, 0, 8)

    def exchange(k, peer_step):
        peer = lax.rem(me + peer_step, n)
        window = pl.ds(first_row[k], part[k])
        return remote(
            send_ref.at[k, window], recv_ref.at[k, me, window],
            all_send_sem.at[k, peer_step], all_recv_sem.at[k, me], peer,
        )

    def send_all(k):
        def go(step, carry):
            exchange(k, step).start()
            return carry

        lax.fori_loop(1, n, go, 0, unroll=n <= 16)
        recv_ref[k, me] = send_ref[k]

    def wait_all(k):
        window = pl.ds(first_row[k], part[k])

        def go(step, carry):
            peer = lax.rem(me + step, n)
            remote(
                send_ref.at[k, window], recv_ref.at[k, peer, window],
                all_send_sem.at[k, step], all_recv_sem.at[k, peer], peer,
            ).wait_recv()
            return carry

        lax.fori_loop(1, n, go, 0, unroll=n <= 16)
        parts = [recv_ref[k, i, first_row[k] : first_row[k] + part[k], :] for i in range(n)]
        while len(parts) > 1:
            parts = [parts[i] + parts[i + 1] for i in range(0, len(parts) - 1, 2)] + (
                [parts[-1]] if len(parts) % 2 else []
            )
        return parts[0]

    def row_up(src, dst, k):
        return remote(src, dst, row_send_sem.at[k], row_recv_sem.at[k], me + 1)

    def row_down(src, dst, k):
        return remote(src, dst, row_send_sem.at[k], row_recv_sem.at[k], me - 1)

    last = pl.ds(rows - 1, 1)
    first = pl.ds(0, 1)
    north_up = row_up(north_ref.at[last], nlo_ref, 0)
    sm_up = row_up(sm_ref.at[last], smlo_ref, 1)
    sm_down = row_down(sm_ref.at[first], smhi_ref, 2)
    q_up = row_up(q_ref.at[last], qlo_ref, 3)
    q_down = row_down(q_ref.at[first], qhi_ref, 4)

    @pl.when(jnp.logical_not(has_down))
    def _():
        for ref in (nlo_ref, smlo_ref, qlo_ref):
            ref[...] = jnp.zeros_like(ref)

    @pl.when(jnp.logical_not(has_up))
    def _():
        for ref in (smhi_ref, qhi_ref):
            ref[...] = jnp.zeros_like(ref)

    loads[0].wait()

    def first_moments(c, carry):
        lift(c, f_ref[:, cols(c)])
        return carry

    lax.fori_loop(0, chunks, first_moments, 0)
    send_ref[0, 0:8] = packed_moments()
    send_ref[0, 8:16] = jnp.zeros((8, LANES), jnp.float32)
    loads[1].wait()
    pl.semaphore_wait(barrier, n - 1)
    send_all(0)

    @pl.when(has_up)
    def _():
        north_up.start()

    loads[2].wait()
    loads[3].wait()
    loads[4].wait()

    for k in range(coarse):
        ct_ref[k] = jnp.concatenate([inv_ref[k]] * 2, axis=1)

    @pl.when(has_down)
    def _():
        north_up.wait_recv()

    def coefficients(c, energy):
        at = cols(c)
        here = line_of(mask_ref.at[0], c)
        raw = east_ref[:, pl.ds(pl.multiple_of(c * span, LANES), span + LANES)]
        e = raw[:, LANES:] * line_of(mask_ref.at[1], c)
        w = pltpu.roll(raw, 1, 1)[:, LANES:] * line_of(mask_ref.at[2], c)
        nf = north_ref[:, at] * jnp.where(row_id == rows - 1, line_of(mask_ref.at[3], c), here)
        sf = jnp.where(
            row_id == 0, nlo_ref[:, at] * line_of(mask_ref.at[4], c), pltpu.roll(nf, 1, 0)
        )
        center = (1.0 - here) + here * storage_ref[:, at] + e + w + nf + sf
        jacobi = 1.0 / center
        f = f_ref[:, at]
        smoothed = jacobi * f
        e_ref[:, at] = e
        w_ref[:, at] = w
        s_ref[:, at] = sf
        c_ref[:, at] = center
        j_ref[:, at] = jacobi
        sm_ref[:, at] = smoothed
        return energy + f * smoothed

    zero = jnp.zeros((rows, span), jnp.float32)

    energy_part = lax.fori_loop(0, chunks, coefficients, zero)

    @pl.when(has_up)
    def _():
        sm_up.start()

    @pl.when(has_down)
    def _():
        sm_down.start()

    def lane_sums(v):
        v = jnp.sum(v, axis=0, keepdims=True)
        return functools.reduce(
            lambda a, b: a + b, [v[:, t * LANES : (t + 1) * LANES] for t in range(BLOCKS)]
        )

    def dots_rows(a, b):
        r = lax.broadcasted_iota(jnp.int32, (8, LANES), 0)
        return jnp.where(r == 0, lane_sums(a), jnp.where(r == 1, lane_sums(b), 0.0))

    def total(block, row):
        return jnp.sum(block[row : row + 1, :], axis=1, keepdims=True)

    def expand(g):
        c = ct_ref[0] * g[0:1, :]
        for k in range(1, coarse):
            c = c + ct_ref[k] * g[k : k + 1, :]
        gc = jnp.sum(jnp.sum(g * c, axis=0, keepdims=True)[:, :half], axis=1, keepdims=True)
        d = dot(c.T, kron_ref[...])
        d = jnp.where(same_half, d, 0.0)
        spread_ref[...] = dot(own_ref[0], d)

        def edge(modes):
            return functools.reduce(
                lambda a, b: a + b,
                [modes[p] * d[:, p * LANES : (p + 1) * LANES] for p in range(ORDER)],
            )

        edge_ref[0] = dot(own_ref[2], edge(down_modes))
        edge_ref[1] = dot(own_ref[3], edge(up_modes))
        return gc

    def spread(c):
        return functools.reduce(
            lambda a, b: a + b,
            [wide(row_modes[p]) * line_of(spread_ref, c, p * LANES) for p in range(ORDER)],
        )

    def wrap(ref):
        ref[:, 0:LANES] = ref[:, width : width + LANES]
        ref[:, width + LANES : width + 2 * LANES] = ref[:, LANES : 2 * LANES]

    def operate(z_ref, c, low, high, nf):
        at = cols(c)
        window = z_ref[:, cols(c, 0, 2 * LANES)]
        size = span + 2 * LANES
        v = window[:, LANES : LANES + span]
        east_v = pltpu.roll(window, size - 1, 1)[:, LANES : LANES + span]
        west_v = pltpu.roll(window, 1, 1)[:, LANES : LANES + span]
        north_v = jnp.where(row_id == rows - 1, high, pltpu.roll(v, rows - 1, 0))
        south_v = jnp.where(row_id == 0, low, pltpu.roll(v, 1, 0))
        image = (
            c_ref[:, at] * v - e_ref[:, at] * east_v - w_ref[:, at] * west_v
            - nf * north_v - s_ref[:, at] * south_v
        )
        return v, image

    g = unpacked(wait_all(0))
    coarse_energy = expand(g)

    def north_of(c):
        return north_ref[:, cols(c)] * jnp.where(
            row_id == rows - 1, line_of(mask_ref.at[3], c), line_of(mask_ref.at[0], c)
        )

    def precondition0(c, carry):
        z0_ref[:, cols(c, LANES)] = sm_ref[:, cols(c)] + spread(c)
        return carry

    lax.fori_loop(0, chunks, precondition0, 0)
    wrap(z0_ref)

    @pl.when(has_down)
    def _():
        sm_up.wait_recv()

    @pl.when(has_up)
    def _():
        sm_down.wait_recv()

    def image0(c, along):
        at = cols(c)
        low = smlo_ref[:, at] + line_of(edge_ref.at[0], c)
        high = smhi_ref[:, at] + line_of(edge_ref.at[1], c)
        v, image = operate(z0_ref, c, low, high, north_of(c))
        im0_ref[:, at] = image
        q_ref[:, at] = j_ref[:, at] * image
        lift(c, image)
        return along + v * image

    along_part = lax.fori_loop(0, chunks, image0, zero)

    @pl.when(has_up)
    def _():
        q_up.start()

    @pl.when(has_down)
    def _():
        q_down.start()

    send_ref[1, 0:8] = packed_moments()
    send_ref[1, 8:16] = dots_rows(energy_part, along_part)
    send_all(1)
    sums = wait_all(1)
    energy = total(sums[8:16], 0) + coarse_energy
    alpha = energy / total(sums[8:16], 1)
    g = g - alpha * unpacked(sums[0:8])
    coarse_energy = expand(g)

    def precondition1(c, acc):
        at = cols(c)
        smoothed = sm_ref[:, at] - alpha * q_ref[:, at]
        residual = f_ref[:, at] - alpha * im0_ref[:, at]
        f_ref[:, at] = residual
        z1_ref[:, cols(c, LANES)] = smoothed + spread(c)
        return acc + residual * smoothed

    energy_part = lax.fori_loop(0, chunks, precondition1, zero)
    wrap(z1_ref)

    @pl.when(has_down)
    def _():
        q_up.wait_recv()

    @pl.when(has_up)
    def _():
        q_down.wait_recv()

    def image1(c, along):
        at = cols(c)
        low = smlo_ref[:, at] - alpha * qlo_ref[:, at] + line_of(edge_ref.at[0], c)
        high = smhi_ref[:, at] - alpha * qhi_ref[:, at] + line_of(edge_ref.at[1], c)
        v, image = operate(z1_ref, c, low, high, north_of(c))
        im1_ref[:, at] = image
        return along + v * image

    along_part = lax.fori_loop(0, chunks, image1, zero)
    send_ref[2, 0:8] = jnp.zeros((8, LANES), jnp.float32)
    send_ref[2, 8:16] = dots_rows(energy_part, along_part)
    send_all(2)
    sums = wait_all(2)
    energy_next = total(sums, 0) + coarse_energy
    beta = energy_next / energy
    alpha_next = energy_next / (total(sums, 1) - beta * energy_next / alpha)

    def finish(c, carry):
        at = cols(c)
        z0 = z0_ref[:, cols(c, LANES)]
        sol_ref[:, at] = alpha * z0 + alpha_next * (z1_ref[:, cols(c, LANES)] + beta * z0)
        res_ref[:, at] = f_ref[:, at] - alpha_next * (im1_ref[:, at] + beta * im0_ref[:, at])
        return carry

    lax.fori_loop(0, chunks, finish, 0)

    @pl.when(has_up)
    def _():
        north_up.wait_send()
        sm_up.wait_send()
        q_up.wait_send()

    @pl.when(has_down)
    def _():
        sm_down.wait_send()
        q_down.wait_send()

    for k in range(3):
        def drain(step, carry):
            exchange(k, step).wait_send()
            return carry

        lax.fori_loop(1, n, drain, 0, unroll=n <= 16)


def body(forcing, east, north, storage, coarse_inverse, membership, land):
    n = lax.axis_size("gy")
    rows, width = forcing.shape
    basins, coarse, _ = coarse_inverse.shape
    inverse = jnp.transpose(coarse_inverse, (1, 2, 0))
    by_row, kron = tables()
    field = pltpu.VMEM((rows, width), jnp.float32)
    padded = pltpu.VMEM((rows, width + 2 * LANES), jnp.float32)
    line = pltpu.VMEM((1, width), jnp.float32)
    blocks = width // LANES
    hbm = pl.BlockSpec(memory_space=pltpu.HBM)
    vmem = pl.BlockSpec(memory_space=pltpu.VMEM)
    return pl.pallas_call(
        functools.partial(kernel, n),
        out_shape=[jax.ShapeDtypeStruct((rows, width), jnp.float32)] * 2,
        in_specs=[hbm] * 4 + [vmem] * 5,
        out_specs=[vmem] * 2,
        scratch_shapes=[
            field, padded, field, field,
            field, field, field, field, field, field, field, padded, padded, field, field,
            pltpu.VMEM((5, blocks, LANES), jnp.float32),
            pltpu.VMEM((4, blocks, LANES), jnp.float32),
            pltpu.VMEM((blocks, ORDER * LANES), jnp.float32),
            pltpu.VMEM((2, blocks, LANES), jnp.float32),
            pltpu.VMEM((blocks, ORDER * LANES), jnp.float32),
            pltpu.VMEM((coarse, coarse, LANES), jnp.float32),
            line, line, line, line, line,
            pltpu.VMEM((3, 16, LANES), jnp.float32),
            pltpu.VMEM((3, n, 16, LANES), jnp.float32),
            pltpu.SemaphoreType.DMA((5,)),
            pltpu.SemaphoreType.DMA((5,)),
            pltpu.SemaphoreType.DMA((5,)),
            pltpu.SemaphoreType.DMA((3, n)),
            pltpu.SemaphoreType.DMA((3, n)),
        ],
        compiler_params=pltpu.CompilerParams(
            collective_id=0, has_side_effects=True, vmem_limit_bytes=VMEM - 8 * rows * width - SPARE
        ),
        name="solve",
    )(forcing, east, north, storage, inverse, membership, land, jnp.asarray(by_row), jnp.asarray(kron))


def solution(mesh):
    return jax.shard_map(
        body,
        mesh=mesh,
        in_specs=(
            P(("ens", "gy"), None),
            P("gy", None),
            P("gy", None),
            P("gy", None),
            P(),
            P(),
            P(),
        ),
        out_specs=(P(("ens", "gy"), None), P(("ens", "gy"), None)),
        check_vma=False,
    )
```

```python
import functools

import jax
import jax.numpy as jnp
import numpy as np
from jax import lax
from jax.experimental import pallas as pl
from jax.experimental.pallas import tpu as pltpu
from jax.sharding import PartitionSpec as P

TILE = 64
ORDER = 4
LANES = 128
BLOCKS = 8
MESH = pl.DeviceIdType.MESH


def tables():
    degree = np.arange(ORDER, dtype=np.float64)
    local = np.arange(TILE, dtype=np.float64)
    modes = np.cos(np.pi * degree[:, None] * (local[None, :] + 0.5) / TILE).astype(np.float32)
    by_row = np.repeat(modes[:, :, None], LANES, axis=2)
    kron = np.zeros((ORDER * ORDER, ORDER * LANES), np.float32)
    for p in range(ORDER):
        for q in range(ORDER):
            kron[p * ORDER + q, p * LANES : (p + 1) * LANES] = np.tile(modes[q], LANES // TILE)
    return by_row, kron


def halves(x):
    high = x.astype(jnp.bfloat16)
    return high, (x - high.astype(jnp.float32)).astype(jnp.bfloat16)


def one_pass(a, b, contract):
    return lax.dot_general(a, b, (contract, ((), ())), preferred_element_type=jnp.float32)


def pick(a, b):
    high, low = halves(b)
    a = a.astype(jnp.bfloat16)
    return one_pass(a, high, ((1,), (0,))) + one_pass(a, low, ((1,), (0,)))


def dot(a, b, contract=((1,), (0,))):
    (ah, al), (bh, bl) = halves(a), halves(b)
    return one_pass(ah, bh, contract) + (one_pass(ah, bl, contract) + one_pass(al, bh, contract))


def kernel(
    n,
    forcing_hbm, east_hbm, north_hbm, storage_hbm, inv_hbm,
    membership_hbm, land_hbm, by_row_hbm, kron_hbm,
    sol_ref, res_ref,
    inv_ref, membership_ref, land_ref, by_row_ref, kron_ref,
    f_ref, east_ref, north_ref, storage_ref,
    e_ref, w_ref, s_ref, c_ref, j_ref, sm_ref, q_ref, z0_ref, z1_ref, im0_ref, im1_ref,
    mask_ref, own_ref, spread_ref, edge_ref, lift_ref, ct_ref,
    nlo_ref, smlo_ref, smhi_ref, qlo_ref, qhi_ref,
    send_ref, recv_ref,
    in_sem, row_send_sem, row_recv_sem, all_send_sem, all_recv_sem,
):
    rows, width = f_ref.shape
    coarse = inv_ref.shape[0]
    blocks = width // LANES
    half = LANES // 2
    span = BLOCKS * LANES
    chunks = width // span
    tile_rows = membership_ref.shape[0]
    me = lax.axis_index("gy")
    start = me * rows
    has_up = me < n - 1
    has_down = me > 0

    def load(src, dst, k):
        return pltpu.make_async_copy(src, dst, in_sem.at[k])

    tables_in = [
        load(membership_hbm, membership_ref, 5),
        load(land_hbm, land_ref, 6),
        load(by_row_hbm, by_row_ref, 7),
        load(kron_hbm, kron_ref, 8),
        load(inv_hbm, inv_ref, 9),
    ]
    loads = [
        load(forcing_hbm, f_ref, 0),
        load(north_hbm, north_ref, 1),
        load(east_hbm, east_ref.at[:, pl.ds(LANES, width)], 2),
        load(east_hbm.at[:, pl.ds(width - LANES, LANES)], east_ref.at[:, pl.ds(0, LANES)], 3),
        load(storage_hbm, storage_ref, 4),
    ]
    for copy in tables_in + loads:
        copy.start()

    barrier = pltpu.get_barrier_semaphore()

    def greet(k, carry):
        pl.semaphore_signal(
            barrier, inc=1, device_id={"gy": lax.rem(me + k, n)}, device_id_type=MESH
        )
        return carry

    lax.fori_loop(1, n, greet, 0)

    for copy in tables_in:
        copy.wait()

    own_row = start // TILE
    up_row = jnp.minimum((start + rows) // TILE, tile_rows - 1)
    down_row = jnp.maximum(start - 1, 0) // TILE
    local_own = pl.multiple_of(lax.rem(start, TILE), rows)
    local_up = lax.rem(start + rows, TILE)
    local_down = lax.rem(start + TILE - 1, TILE)

    tiles = membership_ref.shape[1]
    tile_id = lax.broadcasted_iota(jnp.int32, (blocks, tiles), 1)
    block_id = lax.broadcasted_iota(jnp.int32, (blocks, tiles), 0)
    even = tile_id == 2 * block_id
    odd = tile_id == 2 * block_id + 1
    lane = lax.broadcasted_iota(jnp.int32, (blocks, LANES), 1)
    left = lane < half
    basin_of_lane = jnp.where(left, lane, lane - half)

    def columns(table, row):
        line = table[pl.ds(row, 1), :].astype(jnp.float32)
        first = jnp.sum(jnp.where(even, line, 0.0), axis=1, keepdims=True)
        second = jnp.sum(jnp.where(odd, line, 0.0), axis=1, keepdims=True)
        return (
            jnp.broadcast_to(first, (blocks, LANES)),
            jnp.broadcast_to(second, (blocks, LANES)),
        )

    def owned(row, wet0, wet1):
        first, second = columns(membership_ref, row)
        which = jnp.where(left, first, second)
        hit = which == basin_of_lane.astype(jnp.float32)
        return jnp.where(hit, jnp.where(left, wet0, wet1), 0.0)

    def wets(row):
        first, second = columns(land_ref, row)
        return 1.0 - first, 1.0 - second

    wet0, wet1 = wets(own_row)
    wet = jnp.where(left, wet0, wet1)
    east_wet = jnp.where(
        lane == half - 1, wet1, jnp.where(lane == LANES - 1, pltpu.roll(wet0, blocks - 1, 0), wet)
    )
    west_wet = jnp.where(lane == 0, pltpu.roll(wet1, 1, 0), jnp.where(lane == half, wet0, wet))
    up0, up1 = wets(up_row)
    down0, down1 = wets(down_row)
    mask_ref[0] = wet
    mask_ref[1] = wet * east_wet
    mask_ref[2] = wet * west_wet
    mask_ref[3] = jnp.where(has_up, wet * jnp.where(left, up0, up1), 0.0)
    mask_ref[4] = jnp.where(has_down, wet * jnp.where(left, down0, down1), 0.0)
    own_ref[0] = owned(own_row, wet0, wet1)
    own_ref[1] = own_ref[0].T
    own_ref[2] = owned(down_row, down0, down1)
    own_ref[3] = owned(up_row, up0, up1)

    row_modes = [by_row_ref[p, pl.ds(local_own, rows), :] for p in range(ORDER)]
    up_modes = [by_row_ref[p, pl.ds(local_up, 1), :] for p in range(ORDER)]
    down_modes = [by_row_ref[p, pl.ds(local_down, 1), :] for p in range(ORDER)]

    def wide(v):
        return jnp.concatenate([v] * BLOCKS, axis=1)

    def group(c):
        return pl.ds(pl.multiple_of(c * BLOCKS, BLOCKS), BLOCKS)

    def line_of(ref, c, lane0=0):
        block = ref[group(c), lane0 : lane0 + LANES]
        return jnp.concatenate([block[t : t + 1, :] for t in range(BLOCKS)], axis=1)

    def cols(c, offset=0, extra=0):
        return pl.ds(pl.multiple_of(c * span + offset, LANES), span + extra)

    row_id = lax.broadcasted_iota(jnp.int32, (rows, span), 0)

    sub = lax.broadcasted_iota(jnp.int32, (8, LANES), 0)

    def sum_rows(parts):
        for bit in (4, 2, 1):
            lower = lax.rem(sub // bit, 2) == 0
            merged = []
            for t in range(bit):
                a, b = parts[t], parts[t + bit]
                other = jnp.where(lower, b, a)
                turned = pltpu.roll(other, 8 - bit, 0)
                if bit != 4:
                    turned = jnp.where(lower, turned, pltpu.roll(other, bit, 0))
                merged.append(jnp.where(lower, a, b) + turned)
            parts = merged
        return parts[0]

    def lift(c, field):
        for p in range(ORDER):
            parts = []
            for t in range(BLOCKS):
                block = field[:, t * LANES : (t + 1) * LANES] * row_modes[p]
                parts.append(functools.reduce(
                    lambda a, b: a + b, [block[i : i + 8] for i in range(0, rows, 8)]
                ))
            lift_ref[group(c), p * LANES : (p + 1) * LANES] = sum_rows(parts)

    half_row = lax.broadcasted_iota(jnp.int32, (LANES, ORDER * LANES), 0) < half
    half_col = (
        lax.rem(lax.broadcasted_iota(jnp.int32, (LANES, ORDER * LANES), 1), LANES) < half
    )
    same_half = half_row == half_col
    left8 = lax.broadcasted_iota(jnp.int32, (coarse // 2, LANES), 1) < half

    def packed_moments():
        sums = pick(own_ref[1], lift_ref[...])
        sums = jnp.where(same_half, sums, 0.0)
        g = dot(kron_ref[...], sums, ((1,), (1,)))
        g = g + pltpu.roll(g, half, 1)
        return jnp.where(left8, g[: coarse // 2], g[coarse // 2 :])

    def unpacked(packed):
        turned = pltpu.roll(packed, half, 1)
        return jnp.concatenate(
            [jnp.where(left8, packed, turned), jnp.where(left8, turned, packed)], axis=0
        )

    def remote(src, dst, send_sem, recv_sem, peer):
        return pltpu.make_async_remote_copy(
            src_ref=src, dst_ref=dst, send_sem=send_sem, recv_sem=recv_sem,
            device_id={"gy": peer}, device_id_type=MESH,
        )

    part = (8, 10, 2)
    first_row = (0, 0, 8)

    def exchange(k, peer_step):
        peer = lax.rem(me + peer_step, n)
        window = pl.ds(first_row[k], part[k])
        return remote(
            send_ref.at[k, window], recv_ref.at[k, me, window],
            all_send_sem.at[k, peer_step], all_recv_sem.at[k, me], peer,
        )

    def send_all(k):
        def go(i, carry):
            step = n // 2 + (2 * (i % 2) - 1) * ((i + 1) // 2)
            exchange(k, step).start()
            return carry

        if n <= 16:
            for i in range(n - 1):
                go(i, 0)
        else:
            lax.fori_loop(0, n - 1, go, 0)
        window = pl.ds(first_row[k], part[k])
        recv_ref[k, me, window] = send_ref[k, window]

    def wait_all(k):
        window = pl.ds(first_row[k], part[k])

        def go(step, carry):
            peer = lax.rem(me + step, n)
            remote(
                send_ref.at[k, window], recv_ref.at[k, peer, window],
                all_send_sem.at[k, step], all_recv_sem.at[k, peer], peer,
            ).wait_recv()
            return carry

        lax.fori_loop(1, n, go, 0, unroll=n <= 16)
        parts = [recv_ref[k, i, first_row[k] : first_row[k] + part[k], :] for i in range(n)]
        while len(parts) > 1:
            parts = [parts[i] + parts[i + 1] for i in range(0, len(parts) - 1, 2)] + (
                [parts[-1]] if len(parts) % 2 else []
            )
        return parts[0]

    def row_up(src, dst, k):
        return remote(src, dst, row_send_sem.at[k], row_recv_sem.at[k], me + 1)

    def row_down(src, dst, k):
        return remote(src, dst, row_send_sem.at[k], row_recv_sem.at[k], me - 1)

    last = pl.ds(rows - 1, 1)
    first = pl.ds(0, 1)
    north_up = row_up(north_ref.at[last], nlo_ref, 0)
    sm_up = row_up(sm_ref.at[last], smlo_ref, 1)
    sm_down = row_down(sm_ref.at[first], smhi_ref, 2)
    q_up = row_up(q_ref.at[last], qlo_ref, 3)
    q_down = row_down(q_ref.at[first], qhi_ref, 4)

    @pl.when(jnp.logical_not(has_down))
    def _():
        for ref in (nlo_ref, smlo_ref, qlo_ref):
            ref[...] = jnp.zeros_like(ref)

    @pl.when(jnp.logical_not(has_up))
    def _():
        for ref in (smhi_ref, qhi_ref):
            ref[...] = jnp.zeros_like(ref)

    loads[0].wait()

    def first_moments(c, carry):
        lift(c, f_ref[:, cols(c)])
        return carry

    lax.fori_loop(0, chunks, first_moments, 0)
    send_ref[0, 0:8] = packed_moments()
    loads[1].wait()
    pl.semaphore_wait(barrier, n - 1)
    send_all(0)

    @pl.when(has_up)
    def _():
        north_up.start()

    loads[2].wait()
    loads[3].wait()
    loads[4].wait()

    for k in range(coarse):
        ct_ref[k] = jnp.concatenate([inv_ref[k]] * 2, axis=1)

    @pl.when(has_down)
    def _():
        north_up.wait_recv()

    def coefficients(c, energy):
        at = cols(c)
        here = line_of(mask_ref.at[0], c)
        raw = east_ref[:, pl.ds(pl.multiple_of(c * span, LANES), span + LANES)]
        e = raw[:, LANES:] * line_of(mask_ref.at[1], c)
        w = pltpu.roll(raw, 1, 1)[:, LANES:] * line_of(mask_ref.at[2], c)
        nf = north_ref[:, at] * jnp.where(row_id == rows - 1, line_of(mask_ref.at[3], c), here)
        sf = jnp.where(
            row_id == 0, nlo_ref[:, at] * line_of(mask_ref.at[4], c), pltpu.roll(nf, 1, 0)
        )
        center = (1.0 - here) + here * storage_ref[:, at] + e + w + nf + sf
        jacobi = 1.0 / center
        f = f_ref[:, at]
        smoothed = jacobi * f
        e_ref[:, at] = e
        w_ref[:, at] = w
        s_ref[:, at] = sf
        c_ref[:, at] = center
        j_ref[:, at] = jacobi
        sm_ref[:, at] = smoothed
        return energy + f * smoothed

    zero = jnp.zeros((rows, span), jnp.float32)

    energy_part = lax.fori_loop(0, chunks, coefficients, zero)

    @pl.when(has_up)
    def _():
        sm_up.start()

    @pl.when(has_down)
    def _():
        sm_down.start()

    def lane_sums(v):
        v = jnp.sum(v, axis=0, keepdims=True)
        return functools.reduce(
            lambda a, b: a + b, [v[:, t * LANES : (t + 1) * LANES] for t in range(BLOCKS)]
        )

    def dots_rows(a, b):
        r = lax.broadcasted_iota(jnp.int32, (8, LANES), 0)
        return jnp.where(r == 0, lane_sums(a), jnp.where(r == 1, lane_sums(b), 0.0))

    def total(block, row):
        return jnp.sum(block[row : row + 1, :], axis=1, keepdims=True)

    def expand(g):
        c = ct_ref[0] * g[0:1, :]
        for k in range(1, coarse):
            c = c + ct_ref[k] * g[k : k + 1, :]
        gc = jnp.sum(jnp.sum(g * c, axis=0, keepdims=True)[:, :half], axis=1, keepdims=True)
        d = dot(c.T, kron_ref[...])
        d = jnp.where(same_half, d, 0.0)
        spread_ref[...] = pick(own_ref[0], d)

        def edge(modes):
            return functools.reduce(
                lambda a, b: a + b,
                [modes[p] * d[:, p * LANES : (p + 1) * LANES] for p in range(ORDER)],
            )

        edge_ref[0] = pick(own_ref[2], edge(down_modes))
        edge_ref[1] = pick(own_ref[3], edge(up_modes))
        return gc

    def spread(c):
        return functools.reduce(
            lambda a, b: a + b,
            [wide(row_modes[p]) * line_of(spread_ref, c, p * LANES) for p in range(ORDER)],
        )

    def wrap(ref):
        ref[:, 0:LANES] = ref[:, width : width + LANES]
        ref[:, width + LANES : width + 2 * LANES] = ref[:, LANES : 2 * LANES]

    def operate(z_ref, c, low, high, nf):
        at = cols(c)
        window = z_ref[:, cols(c, 0, 2 * LANES)]
        size = span + 2 * LANES
        v = window[:, LANES : LANES + span]
        east_v = pltpu.roll(window, size - 1, 1)[:, LANES : LANES + span]
        west_v = pltpu.roll(window, 1, 1)[:, LANES : LANES + span]
        north_v = jnp.where(row_id == rows - 1, high, pltpu.roll(v, rows - 1, 0))
        south_v = jnp.where(row_id == 0, low, pltpu.roll(v, 1, 0))
        image = (
            c_ref[:, at] * v - e_ref[:, at] * east_v - w_ref[:, at] * west_v
            - nf * north_v - s_ref[:, at] * south_v
        )
        return v, image

    g = unpacked(wait_all(0))
    coarse_energy = expand(g)

    def north_of(c):
        return north_ref[:, cols(c)] * jnp.where(
            row_id == rows - 1, line_of(mask_ref.at[3], c), line_of(mask_ref.at[0], c)
        )

    def precondition0(c, carry):
        z0_ref[:, cols(c, LANES)] = sm_ref[:, cols(c)] + spread(c)
        return carry

    lax.fori_loop(0, chunks, precondition0, 0)
    wrap(z0_ref)

    @pl.when(has_down)
    def _():
        sm_up.wait_recv()

    @pl.when(has_up)
    def _():
        sm_down.wait_recv()

    def image0(c, along):
        at = cols(c)
        low = smlo_ref[:, at] + line_of(edge_ref.at[0], c)
        high = smhi_ref[:, at] + line_of(edge_ref.at[1], c)
        v, image = operate(z0_ref, c, low, high, north_of(c))
        im0_ref[:, at] = image
        q_ref[:, at] = j_ref[:, at] * image
        lift(c, image)
        return along + v * image

    along_part = lax.fori_loop(0, chunks, image0, zero)

    @pl.when(has_up)
    def _():
        q_up.start()

    @pl.when(has_down)
    def _():
        q_down.start()

    send_ref[1, 0:8] = packed_moments()
    send_ref[1, 8:16] = dots_rows(energy_part, along_part)
    send_all(1)
    sums = wait_all(1)
    energy = total(sums, 8) + coarse_energy
    alpha = energy / total(sums, 9)
    g = g - alpha * unpacked(sums[0:8])
    coarse_energy = expand(g)

    def precondition1(c, acc):
        at = cols(c)
        smoothed = sm_ref[:, at] - alpha * q_ref[:, at]
        residual = f_ref[:, at] - alpha * im0_ref[:, at]
        f_ref[:, at] = residual
        z1_ref[:, cols(c, LANES)] = smoothed + spread(c)
        return acc + residual * smoothed

    energy_part = lax.fori_loop(0, chunks, precondition1, zero)
    wrap(z1_ref)

    @pl.when(has_down)
    def _():
        q_up.wait_recv()

    @pl.when(has_up)
    def _():
        q_down.wait_recv()

    def image1(c, along):
        at = cols(c)
        low = smlo_ref[:, at] - alpha * qlo_ref[:, at] + line_of(edge_ref.at[0], c)
        high = smhi_ref[:, at] - alpha * qhi_ref[:, at] + line_of(edge_ref.at[1], c)
        v, image = operate(z1_ref, c, low, high, north_of(c))
        im1_ref[:, at] = image
        return along + v * image

    along_part = lax.fori_loop(0, chunks, image1, zero)
    send_ref[2, 8:16] = dots_rows(energy_part, along_part)
    send_all(2)
    sums = wait_all(2)
    energy_next = total(sums, 0) + coarse_energy
    beta = energy_next / energy
    alpha_next = energy_next / (total(sums, 1) - beta * energy_next / alpha)

    def finish(c, carry):
        at = cols(c)
        z0 = z0_ref[:, cols(c, LANES)]
        sol_ref[:, at] = alpha * z0 + alpha_next * (z1_ref[:, cols(c, LANES)] + beta * z0)
        res_ref[:, at] = f_ref[:, at] - alpha_next * (im1_ref[:, at] + beta * im0_ref[:, at])
        return carry

    lax.fori_loop(0, chunks, finish, 0)

    @pl.when(has_up)
    def _():
        north_up.wait_send()
        sm_up.wait_send()
        q_up.wait_send()

    @pl.when(has_down)
    def _():
        sm_down.wait_send()
        q_down.wait_send()

    for k in range(3):
        def drain(step, carry):
            exchange(k, step).wait_send()
            return carry

        lax.fori_loop(1, n, drain, 0, unroll=n <= 16)


def body(forcing, east, north, storage, coarse_inverse, membership, land):
    n = lax.axis_size("gy")
    rows, width = forcing.shape
    basins, coarse, _ = coarse_inverse.shape
    inverse = jnp.transpose(coarse_inverse, (1, 2, 0))
    by_row, kron = tables()
    field = pltpu.VMEM((rows, width), jnp.float32)
    padded = pltpu.VMEM((rows, width + 2 * LANES), jnp.float32)
    line = pltpu.VMEM((1, width), jnp.float32)
    blocks = width // LANES
    hbm = pl.BlockSpec(memory_space=pltpu.HBM)
    vmem = pl.BlockSpec(memory_space=pltpu.VMEM)
    return pl.pallas_call(
        functools.partial(kernel, n),
        out_shape=[jax.ShapeDtypeStruct((rows, width), jnp.float32)] * 2,
        in_specs=[hbm] * 9,
        out_specs=[vmem] * 2,
        scratch_shapes=[
            pltpu.VMEM((coarse, coarse, basins), jnp.float32),
            pltpu.VMEM(membership.shape, jnp.int32),
            pltpu.VMEM(land.shape, jnp.int32),
            pltpu.VMEM(by_row.shape, jnp.float32),
            pltpu.VMEM(kron.shape, jnp.float32),
            field, padded, field, field,
            field, field, field, field, field, field, field, padded, padded, field, field,
            pltpu.VMEM((5, blocks, LANES), jnp.float32),
            pltpu.VMEM((4, blocks, LANES), jnp.float32),
            pltpu.VMEM((blocks, ORDER * LANES), jnp.float32),
            pltpu.VMEM((2, blocks, LANES), jnp.float32),
            pltpu.VMEM((blocks, ORDER * LANES), jnp.float32),
            pltpu.VMEM((coarse, coarse, LANES), jnp.float32),
            line, line, line, line, line,
            pltpu.VMEM((3, 16, LANES), jnp.float32),
            pltpu.VMEM((3, n, 16, LANES), jnp.float32),
            pltpu.SemaphoreType.DMA((10,)),
            pltpu.SemaphoreType.DMA((5,)),
            pltpu.SemaphoreType.DMA((5,)),
            pltpu.SemaphoreType.DMA((3, n)),
            pltpu.SemaphoreType.DMA((3, n)),
        ],
        compiler_params=pltpu.CompilerParams(
            collective_id=0, has_side_effects=True, vmem_limit_bytes=48 * 1024 * 1024
        ),
        name="solve",
    )(*(
        pltpu.with_memory_space_constraint(x, pltpu.HBM)
        for x in (
            forcing, east, north, storage, inverse, membership, land,
            jnp.asarray(by_row), jnp.asarray(kron),
        )
    ))


def solution(mesh):
    return jax.shard_map(
        body,
        mesh=mesh,
        in_specs=(
            P(("ens", "gy"), None),
            P("gy", None),
            P("gy", None),
            P("gy", None),
            P(),
            P(),
            P(),
        ),
        out_specs=(P(("ens", "gy"), None), P(("ens", "gy"), None)),
        check_vma=False,
    )
```

```python
import functools

import jax
import jax.numpy as jnp
import numpy as np
from jax import lax
from jax.experimental import pallas as pl
from jax.experimental.pallas import tpu as pltpu
from jax.sharding import PartitionSpec as P

TILE = 64
ORDER = 4
LANES = 128
BLOCKS = 8
MESH = pl.DeviceIdType.MESH


def tables():
    degree = np.arange(ORDER, dtype=np.float64)
    local = np.arange(TILE, dtype=np.float64)
    modes = np.cos(np.pi * degree[:, None] * (local[None, :] + 0.5) / TILE).astype(np.float32)
    by_row = np.repeat(modes[:, :, None], LANES, axis=2)
    kron = np.zeros((ORDER * ORDER, ORDER * LANES), np.float32)
    for p in range(ORDER):
        for q in range(ORDER):
            kron[p * ORDER + q, p * LANES : (p + 1) * LANES] = np.tile(modes[q], LANES // TILE)
    return by_row, kron


def halves(x):
    high = x.astype(jnp.bfloat16)
    return high, (x - high.astype(jnp.float32)).astype(jnp.bfloat16)


def one_pass(a, b, contract):
    return lax.dot_general(a, b, (contract, ((), ())), preferred_element_type=jnp.float32)


def pick(a, b):
    high, low = halves(b)
    a = a.astype(jnp.bfloat16)
    return one_pass(a, high, ((1,), (0,))) + one_pass(a, low, ((1,), (0,)))


def dot(a, b, contract=((1,), (0,))):
    (ah, al), (bh, bl) = halves(a), halves(b)
    return one_pass(ah, bh, contract) + (one_pass(ah, bl, contract) + one_pass(al, bh, contract))


def kernel(
    n,
    forcing_hbm, east_hbm, north_hbm, storage_hbm, inv_hbm,
    membership_hbm, land_hbm, by_row_hbm, kron_hbm,
    sol_ref, res_ref,
    inv_ref, membership_ref, land_ref, by_row_ref, kron_ref,
    f_ref, east_ref, north_ref, storage_ref,
    e_ref, w_ref, s_ref, c_ref, j_ref, sm_ref, q_ref, z0_ref, z1_ref, im0_ref, im1_ref, n_ref,
    mask_ref, own_ref, spread_ref, edge_ref, lift_ref, ct_ref,
    nlo_ref, smlo_ref, smhi_ref, qlo_ref, qhi_ref,
    send_ref, recv_ref,
    in_sem, row_send_sem, row_recv_sem, all_send_sem, all_recv_sem,
):
    rows, width = f_ref.shape
    coarse = inv_ref.shape[0]
    blocks = width // LANES
    half = LANES // 2
    span = BLOCKS * LANES
    chunks = width // span
    tile_rows = membership_ref.shape[0]
    me = lax.axis_index("gy")
    start = me * rows
    has_up = me < n - 1
    has_down = me > 0

    def load(src, dst, k):
        return pltpu.make_async_copy(src, dst, in_sem.at[k])

    tables_in = [
        load(membership_hbm, membership_ref, 5),
        load(land_hbm, land_ref, 6),
        load(by_row_hbm, by_row_ref, 7),
        load(kron_hbm, kron_ref, 8),
        load(inv_hbm, inv_ref, 9),
    ]
    loads = [
        load(forcing_hbm, f_ref, 0),
        load(north_hbm, north_ref, 1),
        load(east_hbm, east_ref.at[:, pl.ds(LANES, width)], 2),
        load(east_hbm.at[:, pl.ds(width - LANES, LANES)], east_ref.at[:, pl.ds(0, LANES)], 3),
        load(storage_hbm, storage_ref, 4),
    ]
    for copy in tables_in + loads:
        copy.start()

    barrier = pltpu.get_barrier_semaphore()

    def greet(k, carry):
        pl.semaphore_signal(
            barrier, inc=1, device_id={"gy": lax.rem(me + k, n)}, device_id_type=MESH
        )
        return carry

    lax.fori_loop(1, n, greet, 0)

    for copy in tables_in:
        copy.wait()

    own_row = start // TILE
    up_row = jnp.minimum((start + rows) // TILE, tile_rows - 1)
    down_row = jnp.maximum(start - 1, 0) // TILE
    local_own = pl.multiple_of(lax.rem(start, TILE), rows)
    local_up = lax.rem(start + rows, TILE)
    local_down = lax.rem(start + TILE - 1, TILE)

    tiles = membership_ref.shape[1]
    tile_id = lax.broadcasted_iota(jnp.int32, (blocks, tiles), 1)
    block_id = lax.broadcasted_iota(jnp.int32, (blocks, tiles), 0)
    even = tile_id == 2 * block_id
    odd = tile_id == 2 * block_id + 1
    lane = lax.broadcasted_iota(jnp.int32, (blocks, LANES), 1)
    left = lane < half
    basin_of_lane = jnp.where(left, lane, lane - half)

    def columns(table, row):
        line = table[pl.ds(row, 1), :].astype(jnp.float32)
        first = jnp.sum(jnp.where(even, line, 0.0), axis=1, keepdims=True)
        second = jnp.sum(jnp.where(odd, line, 0.0), axis=1, keepdims=True)
        return (
            jnp.broadcast_to(first, (blocks, LANES)),
            jnp.broadcast_to(second, (blocks, LANES)),
        )

    def owned(row, wet0, wet1):
        first, second = columns(membership_ref, row)
        which = jnp.where(left, first, second)
        hit = which == basin_of_lane.astype(jnp.float32)
        return jnp.where(hit, jnp.where(left, wet0, wet1), 0.0)

    def wets(row):
        first, second = columns(land_ref, row)
        return 1.0 - first, 1.0 - second

    wet0, wet1 = wets(own_row)
    wet = jnp.where(left, wet0, wet1)
    own_ref[0] = owned(own_row, wet0, wet1)
    own_ref[1] = own_ref[0].T
    row_modes = [by_row_ref[p, pl.ds(local_own, rows), :] for p in range(ORDER)]
    up_modes = [by_row_ref[p, pl.ds(local_up, 1), :] for p in range(ORDER)]
    down_modes = [by_row_ref[p, pl.ds(local_down, 1), :] for p in range(ORDER)]

    def wide(v):
        return jnp.concatenate([v] * BLOCKS, axis=1)

    def group(c):
        return pl.ds(pl.multiple_of(c * BLOCKS, BLOCKS), BLOCKS)

    def line_of(ref, c, lane0=0):
        block = ref[group(c), lane0 : lane0 + LANES]
        return jnp.concatenate([block[t : t + 1, :] for t in range(BLOCKS)], axis=1)

    def cols(c, offset=0, extra=0):
        return pl.ds(pl.multiple_of(c * span + offset, LANES), span + extra)

    row_id = lax.broadcasted_iota(jnp.int32, (rows, span), 0)

    sub = lax.broadcasted_iota(jnp.int32, (8, LANES), 0)

    def sum_rows(parts):
        for bit in (4, 2, 1):
            lower = lax.rem(sub // bit, 2) == 0
            merged = []
            for t in range(bit):
                a, b = parts[t], parts[t + bit]
                other = jnp.where(lower, b, a)
                turned = pltpu.roll(other, 8 - bit, 0)
                if bit != 4:
                    turned = jnp.where(lower, turned, pltpu.roll(other, bit, 0))
                merged.append(jnp.where(lower, a, b) + turned)
            parts = merged
        return parts[0]

    def lift(c, field):
        for p in range(ORDER):
            parts = []
            for t in range(BLOCKS):
                block = field[:, t * LANES : (t + 1) * LANES] * row_modes[p]
                parts.append(functools.reduce(
                    lambda a, b: a + b, [block[i : i + 8] for i in range(0, rows, 8)]
                ))
            lift_ref[group(c), p * LANES : (p + 1) * LANES] = sum_rows(parts)

    half_row = lax.broadcasted_iota(jnp.int32, (LANES, ORDER * LANES), 0) < half
    half_col = (
        lax.rem(lax.broadcasted_iota(jnp.int32, (LANES, ORDER * LANES), 1), LANES) < half
    )
    same_half = half_row == half_col
    left8 = lax.broadcasted_iota(jnp.int32, (coarse // 2, LANES), 1) < half

    def packed_moments():
        sums = pick(own_ref[1], lift_ref[...])
        sums = jnp.where(same_half, sums, 0.0)
        g = dot(kron_ref[...], sums, ((1,), (1,)))
        g = g + pltpu.roll(g, half, 1)
        return jnp.where(left8, g[: coarse // 2], g[coarse // 2 :])

    def unpacked(packed):
        turned = pltpu.roll(packed, half, 1)
        return jnp.concatenate(
            [jnp.where(left8, packed, turned), jnp.where(left8, turned, packed)], axis=0
        )

    def remote(src, dst, send_sem, recv_sem, peer):
        return pltpu.make_async_remote_copy(
            src_ref=src, dst_ref=dst, send_sem=send_sem, recv_sem=recv_sem,
            device_id={"gy": peer}, device_id_type=MESH,
        )

    part = (8, 10, 2)
    first_row = (0, 0, 8)

    def exchange(k, peer_step):
        peer = lax.rem(me + peer_step, n)
        window = pl.ds(first_row[k], part[k])
        return remote(
            send_ref.at[k, window], recv_ref.at[k, me, window],
            all_send_sem.at[k, peer_step], all_recv_sem.at[k, me], peer,
        )

    def send_all(k):
        def go(i, carry):
            step = n // 2 + (2 * (i % 2) - 1) * ((i + 1) // 2)
            exchange(k, step).start()
            return carry

        if n <= 16:
            for i in range(n - 1):
                go(i, 0)
        else:
            lax.fori_loop(0, n - 1, go, 0)
        window = pl.ds(first_row[k], part[k])
        recv_ref[k, me, window] = send_ref[k, window]

    def wait_all(k):
        window = pl.ds(first_row[k], part[k])

        def go(step, carry):
            peer = lax.rem(me + step, n)
            remote(
                send_ref.at[k, window], recv_ref.at[k, peer, window],
                all_send_sem.at[k, step], all_recv_sem.at[k, peer], peer,
            ).wait_recv()
            return carry

        lax.fori_loop(1, n, go, 0, unroll=n <= 16)
        parts = [recv_ref[k, i, first_row[k] : first_row[k] + part[k], :] for i in range(n)]
        while len(parts) > 1:
            parts = [parts[i] + parts[i + 1] for i in range(0, len(parts) - 1, 2)] + (
                [parts[-1]] if len(parts) % 2 else []
            )
        return parts[0]

    def drain(k):
        def go(step, carry):
            exchange(k, step).wait_send()
            return carry

        lax.fori_loop(1, n, go, 0, unroll=n <= 16)

    def row_up(src, dst, k):
        return remote(src, dst, row_send_sem.at[k], row_recv_sem.at[k], me + 1)

    def row_down(src, dst, k):
        return remote(src, dst, row_send_sem.at[k], row_recv_sem.at[k], me - 1)

    last = pl.ds(rows - 1, 1)
    first = pl.ds(0, 1)
    north_up = row_up(north_ref.at[last], nlo_ref, 0)
    sm_up = row_up(sm_ref.at[last], smlo_ref, 1)
    sm_down = row_down(sm_ref.at[first], smhi_ref, 2)
    q_up = row_up(q_ref.at[last], qlo_ref, 3)
    q_down = row_down(q_ref.at[first], qhi_ref, 4)

    @pl.when(jnp.logical_not(has_down))
    def _():
        for ref in (nlo_ref, smlo_ref, qlo_ref):
            ref[...] = jnp.zeros_like(ref)

    @pl.when(jnp.logical_not(has_up))
    def _():
        for ref in (smhi_ref, qhi_ref):
            ref[...] = jnp.zeros_like(ref)

    loads[0].wait()

    def first_moments(c, carry):
        lift(c, f_ref[:, cols(c)])
        return carry

    lax.fori_loop(0, chunks, first_moments, 0)
    send_ref[0, 0:8] = packed_moments()
    loads[1].wait()
    pl.semaphore_wait(barrier, n - 1)
    send_all(0)

    @pl.when(has_up)
    def _():
        north_up.start()

    east_wet = jnp.where(
        lane == half - 1, wet1, jnp.where(lane == LANES - 1, pltpu.roll(wet0, blocks - 1, 0), wet)
    )
    west_wet = jnp.where(lane == 0, pltpu.roll(wet1, 1, 0), jnp.where(lane == half, wet0, wet))
    up0, up1 = wets(up_row)
    down0, down1 = wets(down_row)
    mask_ref[0] = wet
    mask_ref[1] = wet * east_wet
    mask_ref[2] = wet * west_wet
    mask_ref[3] = jnp.where(has_up, wet * jnp.where(left, up0, up1), 0.0)
    mask_ref[4] = jnp.where(has_down, wet * jnp.where(left, down0, down1), 0.0)
    own_ref[2] = owned(down_row, down0, down1)
    own_ref[3] = owned(up_row, up0, up1)

    loads[2].wait()
    loads[3].wait()
    loads[4].wait()

    for k in range(coarse):
        ct_ref[k] = jnp.concatenate([inv_ref[k]] * 2, axis=1)

    @pl.when(has_down)
    def _():
        north_up.wait_recv()

    zero = jnp.zeros((8, LANES), jnp.float32)

    def fold(v):
        parts = [
            v[i : i + 8, t * LANES : (t + 1) * LANES]
            for i in range(0, rows, 8)
            for t in range(BLOCKS)
        ]
        while len(parts) > 1:
            parts = [parts[i] + parts[i + 1] for i in range(0, len(parts), 2)]
        return parts[0]

    def coefficients(c, energy):
        at = cols(c)
        here = line_of(mask_ref.at[0], c)
        raw = east_ref[:, pl.ds(pl.multiple_of(c * span, LANES), span + LANES)]
        e = raw[:, LANES:] * line_of(mask_ref.at[1], c)
        w = pltpu.roll(raw, 1, 1)[:, LANES:] * line_of(mask_ref.at[2], c)
        nf = north_ref[:, at] * jnp.where(row_id == rows - 1, line_of(mask_ref.at[3], c), here)
        sf = jnp.where(
            row_id == 0, nlo_ref[:, at] * line_of(mask_ref.at[4], c), pltpu.roll(nf, 1, 0)
        )
        center = (1.0 - here) + here * storage_ref[:, at] + e + w + nf + sf
        jacobi = 1.0 / center
        f = f_ref[:, at]
        smoothed = jacobi * f
        e_ref[:, at] = e
        w_ref[:, at] = w
        s_ref[:, at] = sf
        n_ref[:, at] = nf
        c_ref[:, at] = center
        j_ref[:, at] = jacobi
        sm_ref[:, at] = smoothed
        return energy + fold(f * smoothed)

    energy_part = lax.fori_loop(0, chunks, coefficients, zero)

    @pl.when(has_up)
    def _():
        sm_up.start()

    @pl.when(has_down)
    def _():
        sm_down.start()

    def lane_sums(v):
        return jnp.sum(v, axis=0, keepdims=True)

    def dots_rows(a, b):
        r = lax.broadcasted_iota(jnp.int32, (8, LANES), 0)
        return jnp.where(r == 0, lane_sums(a), jnp.where(r == 1, lane_sums(b), 0.0))

    def total(block, row):
        return jnp.sum(block[row : row + 1, :], axis=1, keepdims=True)

    def expand(g):
        c = ct_ref[0] * g[0:1, :]
        for k in range(1, coarse):
            c = c + ct_ref[k] * g[k : k + 1, :]
        gc = jnp.sum(jnp.sum(g * c, axis=0, keepdims=True)[:, :half], axis=1, keepdims=True)
        d = dot(c.T, kron_ref[...])
        d = jnp.where(same_half, d, 0.0)
        spread_ref[...] = pick(own_ref[0], d)

        def edge(modes):
            return functools.reduce(
                lambda a, b: a + b,
                [modes[p] * d[:, p * LANES : (p + 1) * LANES] for p in range(ORDER)],
            )

        edge_ref[0] = pick(own_ref[2], edge(down_modes))
        edge_ref[1] = pick(own_ref[3], edge(up_modes))
        return gc

    def spread(c):
        return functools.reduce(
            lambda a, b: a + b,
            [wide(row_modes[p]) * line_of(spread_ref, c, p * LANES) for p in range(ORDER)],
        )

    def wrap(ref):
        ref[:, 0:LANES] = ref[:, width : width + LANES]
        ref[:, width + LANES : width + 2 * LANES] = ref[:, LANES : 2 * LANES]

    def operate(z_ref, c, low, high):
        at = cols(c)
        window = z_ref[:, cols(c, 0, 2 * LANES)]
        size = span + 2 * LANES
        v = window[:, LANES : LANES + span]
        east_v = pltpu.roll(window, size - 1, 1)[:, LANES : LANES + span]
        west_v = pltpu.roll(window, 1, 1)[:, LANES : LANES + span]
        north_v = jnp.where(row_id == rows - 1, high, pltpu.roll(v, rows - 1, 0))
        south_v = jnp.where(row_id == 0, low, pltpu.roll(v, 1, 0))
        image = (
            c_ref[:, at] * v - e_ref[:, at] * east_v - w_ref[:, at] * west_v
            - n_ref[:, at] * north_v - s_ref[:, at] * south_v
        )
        return v, image

    g = unpacked(wait_all(0))
    coarse_energy = expand(g)

    def precondition0(c, carry):
        z0_ref[:, cols(c, LANES)] = sm_ref[:, cols(c)] + spread(c)
        return carry

    lax.fori_loop(0, chunks, precondition0, 0)
    wrap(z0_ref)

    @pl.when(has_down)
    def _():
        sm_up.wait_recv()

    @pl.when(has_up)
    def _():
        sm_down.wait_recv()

    def image0(c, along):
        at = cols(c)
        low = smlo_ref[:, at] + line_of(edge_ref.at[0], c)
        high = smhi_ref[:, at] + line_of(edge_ref.at[1], c)
        v, image = operate(z0_ref, c, low, high)
        im0_ref[:, at] = image
        q_ref[:, at] = j_ref[:, at] * image
        lift(c, image)
        return along + fold(v * image)

    along_part = lax.fori_loop(0, chunks, image0, zero)

    @pl.when(has_up)
    def _():
        q_up.start()

    @pl.when(has_down)
    def _():
        q_down.start()

    send_ref[1, 0:8] = packed_moments()
    send_ref[1, 8:16] = dots_rows(energy_part, along_part)
    send_all(1)
    drain(0)
    sums = wait_all(1)
    energy = total(sums, 8) + coarse_energy
    alpha = energy / total(sums, 9)
    g = g - alpha * unpacked(sums[0:8])
    coarse_energy = expand(g)

    def precondition1(c, acc):
        at = cols(c)
        smoothed = sm_ref[:, at] - alpha * q_ref[:, at]
        residual = f_ref[:, at] - alpha * im0_ref[:, at]
        f_ref[:, at] = residual
        z1_ref[:, cols(c, LANES)] = smoothed + spread(c)
        return acc + fold(residual * smoothed)

    energy_part = lax.fori_loop(0, chunks, precondition1, zero)
    wrap(z1_ref)

    @pl.when(has_down)
    def _():
        q_up.wait_recv()

    @pl.when(has_up)
    def _():
        q_down.wait_recv()

    def image1(c, along):
        at = cols(c)
        low = smlo_ref[:, at] - alpha * qlo_ref[:, at] + line_of(edge_ref.at[0], c)
        high = smhi_ref[:, at] - alpha * qhi_ref[:, at] + line_of(edge_ref.at[1], c)
        v, image = operate(z1_ref, c, low, high)
        im1_ref[:, at] = image
        return along + fold(v * image)

    along_part = lax.fori_loop(0, chunks, image1, zero)
    send_ref[2, 8:16] = dots_rows(energy_part, along_part)
    send_all(2)
    drain(1)
    sums = wait_all(2)
    energy_next = total(sums, 0) + coarse_energy
    beta = energy_next / energy
    alpha_next = energy_next / (total(sums, 1) - beta * energy_next / alpha)

    def finish(c, carry):
        at = cols(c)
        z0 = z0_ref[:, cols(c, LANES)]
        sol_ref[:, at] = alpha * z0 + alpha_next * (z1_ref[:, cols(c, LANES)] + beta * z0)
        res_ref[:, at] = f_ref[:, at] - alpha_next * (im1_ref[:, at] + beta * im0_ref[:, at])
        return carry

    lax.fori_loop(0, chunks, finish, 0)

    @pl.when(has_up)
    def _():
        north_up.wait_send()
        sm_up.wait_send()
        q_up.wait_send()

    @pl.when(has_down)
    def _():
        sm_down.wait_send()
        q_down.wait_send()

    drain(2)


def body(forcing, east, north, storage, coarse_inverse, membership, land):
    n = lax.axis_size("gy")
    rows, width = forcing.shape
    basins, coarse, _ = coarse_inverse.shape
    inverse = jnp.transpose(coarse_inverse, (1, 2, 0))
    by_row, kron = tables()
    field = pltpu.VMEM((rows, width), jnp.float32)
    padded = pltpu.VMEM((rows, width + 2 * LANES), jnp.float32)
    line = pltpu.VMEM((1, width), jnp.float32)
    blocks = width // LANES
    hbm = pl.BlockSpec(memory_space=pltpu.HBM)
    vmem = pl.BlockSpec(memory_space=pltpu.VMEM)
    return pl.pallas_call(
        functools.partial(kernel, n),
        out_shape=[jax.ShapeDtypeStruct((rows, width), jnp.float32)] * 2,
        in_specs=[hbm] * 9,
        out_specs=[vmem] * 2,
        scratch_shapes=[
            pltpu.VMEM((coarse, coarse, basins), jnp.float32),
            pltpu.VMEM(membership.shape, jnp.int32),
            pltpu.VMEM(land.shape, jnp.int32),
            pltpu.VMEM(by_row.shape, jnp.float32),
            pltpu.VMEM(kron.shape, jnp.float32),
            field, padded, field, field,
            field, field, field, field, field, field, field, padded, padded, field, field, field,
            pltpu.VMEM((5, blocks, LANES), jnp.float32),
            pltpu.VMEM((4, blocks, LANES), jnp.float32),
            pltpu.VMEM((blocks, ORDER * LANES), jnp.float32),
            pltpu.VMEM((2, blocks, LANES), jnp.float32),
            pltpu.VMEM((blocks, ORDER * LANES), jnp.float32),
            pltpu.VMEM((coarse, coarse, LANES), jnp.float32),
            line, line, line, line, line,
            pltpu.VMEM((3, 16, LANES), jnp.float32),
            pltpu.VMEM((3, n, 16, LANES), jnp.float32),
            pltpu.SemaphoreType.DMA((10,)),
            pltpu.SemaphoreType.DMA((5,)),
            pltpu.SemaphoreType.DMA((5,)),
            pltpu.SemaphoreType.DMA((3, n)),
            pltpu.SemaphoreType.DMA((3, n)),
        ],
        compiler_params=pltpu.CompilerParams(
            collective_id=0, has_side_effects=True, vmem_limit_bytes=48 * 1024 * 1024
        ),
        name="solve",
    )(*(
        pltpu.with_memory_space_constraint(x, pltpu.HBM)
        for x in (
            forcing, east, north, storage, inverse, membership, land,
            jnp.asarray(by_row), jnp.asarray(kron),
        )
    ))


def solution(mesh):
    return jax.shard_map(
        body,
        mesh=mesh,
        in_specs=(
            P(("ens", "gy"), None),
            P("gy", None),
            P("gy", None),
            P("gy", None),
            P(),
            P(),
            P(),
        ),
        out_specs=(P(("ens", "gy"), None), P(("ens", "gy"), None)),
        check_vma=False,
    )
```

```python
import functools

import jax
import jax.numpy as jnp
import numpy as np
from jax import lax
from jax.experimental import pallas as pl
from jax.experimental.pallas import tpu as pltpu
from jax.sharding import PartitionSpec as P

TILE = 64
ORDER = 4
LANES = 128
BLOCKS = 8
MESH = pl.DeviceIdType.MESH


def tables():
    degree = np.arange(ORDER, dtype=np.float64)
    local = np.arange(TILE, dtype=np.float64)
    modes = np.cos(np.pi * degree[:, None] * (local[None, :] + 0.5) / TILE).astype(np.float32)
    by_row = np.repeat(modes[:, :, None], LANES, axis=2)
    kron = np.zeros((ORDER * ORDER, ORDER * LANES), np.float32)
    for p in range(ORDER):
        for q in range(ORDER):
            kron[p * ORDER + q, p * LANES : (p + 1) * LANES] = np.tile(modes[q], LANES // TILE)
    return by_row, kron


def halves(x):
    high = x.astype(jnp.bfloat16)
    return high, (x - high.astype(jnp.float32)).astype(jnp.bfloat16)


def one_pass(a, b, contract):
    return lax.dot_general(a, b, (contract, ((), ())), preferred_element_type=jnp.float32)


def pick(a, b):
    high, low = halves(b)
    a = a.astype(jnp.bfloat16)
    return one_pass(a, high, ((1,), (0,))) + one_pass(a, low, ((1,), (0,)))


def dot(a, b, contract=((1,), (0,))):
    (ah, al), (bh, bl) = halves(a), halves(b)
    return one_pass(ah, bh, contract) + (one_pass(ah, bl, contract) + one_pass(al, bh, contract))


def kernel(
    n,
    forcing_hbm, east_hbm, north_hbm, storage_hbm, inv_hbm,
    membership_hbm, land_hbm, by_row_hbm, kron_hbm,
    sol_ref, res_ref,
    inv_ref, membership_ref, land_ref, by_row_ref, kron_ref,
    f_ref, east_ref, north_ref, storage_ref,
    e_ref, w_ref, s_ref, c_ref, j_ref, sm_ref, q_ref, z0_ref, z1_ref, im0_ref, im1_ref, n_ref,
    mask_ref, own_ref, spread_ref, edge_ref, lift_ref, ct_ref,
    nlo_ref, smlo_ref, smhi_ref, qlo_ref, qhi_ref,
    send_ref, recv_ref,
    in_sem, row_send_sem, row_recv_sem, all_send_sem, all_recv_sem,
):
    rows, width = f_ref.shape
    coarse = inv_ref.shape[0]
    blocks = width // LANES
    half = LANES // 2
    span = BLOCKS * LANES
    chunks = width // span
    tile_rows = membership_ref.shape[0]
    me = lax.axis_index("gy")
    start = me * rows
    has_up = me < n - 1
    has_down = me > 0

    def load(src, dst, k):
        return pltpu.make_async_copy(src, dst, in_sem.at[k])

    tables_in = [
        load(membership_hbm, membership_ref, 5),
        load(land_hbm, land_ref, 6),
        load(by_row_hbm, by_row_ref, 7),
        load(kron_hbm, kron_ref, 8),
        load(inv_hbm, inv_ref, 9),
    ]
    loads = [
        load(forcing_hbm, f_ref, 0),
        load(north_hbm, north_ref, 1),
        load(east_hbm, east_ref.at[:, pl.ds(LANES, width)], 2),
        load(east_hbm.at[:, pl.ds(width - LANES, LANES)], east_ref.at[:, pl.ds(0, LANES)], 3),
        load(storage_hbm, storage_ref, 4),
    ]
    for copy in tables_in + loads:
        copy.start()

    barrier = pltpu.get_barrier_semaphore()

    def greet(k, carry):
        pl.semaphore_signal(
            barrier, inc=1, device_id={"gy": lax.rem(me + k, n)}, device_id_type=MESH
        )
        return carry

    lax.fori_loop(1, n, greet, 0)

    for copy in tables_in:
        copy.wait()

    own_row = start // TILE
    up_row = jnp.minimum((start + rows) // TILE, tile_rows - 1)
    down_row = jnp.maximum(start - 1, 0) // TILE
    local_own = pl.multiple_of(lax.rem(start, TILE), rows)
    local_up = lax.rem(start + rows, TILE)
    local_down = lax.rem(start + TILE - 1, TILE)

    tiles = membership_ref.shape[1]
    tile_id = lax.broadcasted_iota(jnp.int32, (blocks, tiles), 1)
    block_id = lax.broadcasted_iota(jnp.int32, (blocks, tiles), 0)
    even = tile_id == 2 * block_id
    odd = tile_id == 2 * block_id + 1
    lane = lax.broadcasted_iota(jnp.int32, (blocks, LANES), 1)
    left = lane < half
    basin_of_lane = jnp.where(left, lane, lane - half)

    def columns(table, row):
        line = table[pl.ds(row, 1), :].astype(jnp.float32)
        first = jnp.sum(jnp.where(even, line, 0.0), axis=1, keepdims=True)
        second = jnp.sum(jnp.where(odd, line, 0.0), axis=1, keepdims=True)
        return (
            jnp.broadcast_to(first, (blocks, LANES)),
            jnp.broadcast_to(second, (blocks, LANES)),
        )

    def owned(row, wet0, wet1):
        first, second = columns(membership_ref, row)
        which = jnp.where(left, first, second)
        hit = which == basin_of_lane.astype(jnp.float32)
        return jnp.where(hit, jnp.where(left, wet0, wet1), 0.0)

    def wets(row):
        first, second = columns(land_ref, row)
        return 1.0 - first, 1.0 - second

    wet0, wet1 = wets(own_row)
    wet = jnp.where(left, wet0, wet1)
    own_ref[0] = owned(own_row, wet0, wet1)
    own_ref[1] = own_ref[0].T
    row_modes = [by_row_ref[p, pl.ds(local_own, rows), :] for p in range(ORDER)]
    up_modes = [by_row_ref[p, pl.ds(local_up, 1), :] for p in range(ORDER)]
    down_modes = [by_row_ref[p, pl.ds(local_down, 1), :] for p in range(ORDER)]

    def wide(v):
        return jnp.concatenate([v] * BLOCKS, axis=1)

    def group(c):
        return pl.ds(pl.multiple_of(c * BLOCKS, BLOCKS), BLOCKS)

    def line_of(ref, c, lane0=0):
        block = ref[group(c), lane0 : lane0 + LANES]
        return jnp.concatenate([block[t : t + 1, :] for t in range(BLOCKS)], axis=1)

    def cols(c, offset=0, extra=0):
        return pl.ds(pl.multiple_of(c * span + offset, LANES), span + extra)

    row_id = lax.broadcasted_iota(jnp.int32, (rows, span), 0)

    sub = lax.broadcasted_iota(jnp.int32, (8, LANES), 0)

    def sum_rows(parts):
        for bit in (4, 2, 1):
            lower = lax.rem(sub // bit, 2) == 0
            merged = []
            for t in range(bit):
                a, b = parts[t], parts[t + bit]
                other = jnp.where(lower, b, a)
                turned = pltpu.roll(other, 8 - bit, 0)
                if bit != 4:
                    turned = jnp.where(lower, turned, pltpu.roll(other, bit, 0))
                merged.append(jnp.where(lower, a, b) + turned)
            parts = merged
        return parts[0]

    def lift(c, field):
        for p in range(ORDER):
            parts = []
            for t in range(BLOCKS):
                block = field[:, t * LANES : (t + 1) * LANES] * row_modes[p]
                parts.append(functools.reduce(
                    lambda a, b: a + b, [block[i : i + 8] for i in range(0, rows, 8)]
                ))
            lift_ref[group(c), p * LANES : (p + 1) * LANES] = sum_rows(parts)

    half_row = lax.broadcasted_iota(jnp.int32, (LANES, ORDER * LANES), 0) < half
    half_col = (
        lax.rem(lax.broadcasted_iota(jnp.int32, (LANES, ORDER * LANES), 1), LANES) < half
    )
    same_half = half_row == half_col
    left8 = lax.broadcasted_iota(jnp.int32, (coarse // 2, LANES), 1) < half

    def packed_moments():
        sums = pick(own_ref[1], lift_ref[...])
        sums = jnp.where(same_half, sums, 0.0)
        g = dot(kron_ref[...], sums, ((1,), (1,)))
        g = g + pltpu.roll(g, half, 1)
        return jnp.where(left8, g[: coarse // 2], g[coarse // 2 :])

    def unpacked(packed):
        turned = pltpu.roll(packed, half, 1)
        return jnp.concatenate(
            [jnp.where(left8, packed, turned), jnp.where(left8, turned, packed)], axis=0
        )

    def remote(src, dst, send_sem, recv_sem, peer):
        return pltpu.make_async_remote_copy(
            src_ref=src, dst_ref=dst, send_sem=send_sem, recv_sem=recv_sem,
            device_id={"gy": peer}, device_id_type=MESH,
        )

    part = (8, 10, 2)
    first_row = (0, 0, 8)

    def exchange(k, peer_step):
        peer = lax.rem(me + peer_step, n)
        window = pl.ds(first_row[k], part[k])
        return remote(
            send_ref.at[k, window], recv_ref.at[k, me, window],
            all_send_sem.at[k, peer_step], all_recv_sem.at[k, me], peer,
        )

    def send_all(k):
        def go(i, carry):
            step = n // 2 + (2 * (i % 2) - 1) * ((i + 1) // 2)
            exchange(k, step).start()
            return carry

        if n <= 16:
            for i in range(n - 1):
                go(i, 0)
        else:
            lax.fori_loop(0, n - 1, go, 0)
        window = pl.ds(first_row[k], part[k])
        recv_ref[k, me, window] = send_ref[k, window]

    def wait_all(k):
        window = pl.ds(first_row[k], part[k])

        def go(step, carry):
            peer = lax.rem(me + step, n)
            remote(
                send_ref.at[k, window], recv_ref.at[k, peer, window],
                all_send_sem.at[k, step], all_recv_sem.at[k, peer], peer,
            ).wait_recv()
            return carry

        lax.fori_loop(1, n, go, 0, unroll=n <= 16)
        parts = [recv_ref[k, i, first_row[k] : first_row[k] + part[k], :] for i in range(n)]
        while len(parts) > 1:
            parts = [parts[i] + parts[i + 1] for i in range(0, len(parts) - 1, 2)] + (
                [parts[-1]] if len(parts) % 2 else []
            )
        return parts[0]

    def drain(k):
        def go(step, carry):
            exchange(k, step).wait_send()
            return carry

        lax.fori_loop(1, n, go, 0, unroll=n <= 16)

    def row_up(src, dst, k):
        return remote(src, dst, row_send_sem.at[k], row_recv_sem.at[k], me + 1)

    def row_down(src, dst, k):
        return remote(src, dst, row_send_sem.at[k], row_recv_sem.at[k], me - 1)

    last = pl.ds(rows - 1, 1)
    first = pl.ds(0, 1)
    north_up = row_up(north_ref.at[last], nlo_ref, 0)
    sm_up = row_up(sm_ref.at[last], smlo_ref, 1)
    sm_down = row_down(sm_ref.at[first], smhi_ref, 2)
    q_up = row_up(q_ref.at[last], qlo_ref, 3)
    q_down = row_down(q_ref.at[first], qhi_ref, 4)

    @pl.when(jnp.logical_not(has_down))
    def _():
        for ref in (nlo_ref, smlo_ref, qlo_ref):
            ref[...] = jnp.zeros_like(ref)

    @pl.when(jnp.logical_not(has_up))
    def _():
        for ref in (smhi_ref, qhi_ref):
            ref[...] = jnp.zeros_like(ref)

    loads[0].wait()

    def first_moments(c, carry):
        lift(c, f_ref[:, cols(c)])
        return carry

    lax.fori_loop(0, chunks, first_moments, 0)
    send_ref[0, 0:8] = packed_moments()
    loads[1].wait()
    pl.semaphore_wait(barrier, n - 1)

    @pl.when(has_up)
    def _():
        north_up.start()

    send_all(0)

    east_wet = jnp.where(
        lane == half - 1, wet1, jnp.where(lane == LANES - 1, pltpu.roll(wet0, blocks - 1, 0), wet)
    )
    west_wet = jnp.where(lane == 0, pltpu.roll(wet1, 1, 0), jnp.where(lane == half, wet0, wet))
    up0, up1 = wets(up_row)
    down0, down1 = wets(down_row)
    mask_ref[0] = wet
    mask_ref[1] = wet * east_wet
    mask_ref[2] = wet * west_wet
    mask_ref[3] = jnp.where(has_up, wet * jnp.where(left, up0, up1), 0.0)
    mask_ref[4] = jnp.where(has_down, wet * jnp.where(left, down0, down1), 0.0)
    own_ref[2] = owned(down_row, down0, down1)
    own_ref[3] = owned(up_row, up0, up1)

    loads[2].wait()
    loads[3].wait()
    loads[4].wait()

    for k in range(coarse):
        ct_ref[k] = jnp.concatenate([inv_ref[k]] * 2, axis=1)


    zero = jnp.zeros((8, LANES), jnp.float32)

    def fold(v):
        parts = [
            v[i : i + 8, t * LANES : (t + 1) * LANES]
            for i in range(0, v.shape[0], 8)
            for t in range(BLOCKS)
        ]
        while len(parts) > 1:
            parts = [parts[i] + parts[i + 1] for i in range(0, len(parts), 2)]
        return parts[0]

    def coefficients(c, energy):
        at = cols(c)
        here = line_of(mask_ref.at[0], c)
        raw = east_ref[:, pl.ds(pl.multiple_of(c * span, LANES), span + LANES)]
        e = raw[:, LANES:] * line_of(mask_ref.at[1], c)
        w = pltpu.roll(raw, 1, 1)[:, LANES:] * line_of(mask_ref.at[2], c)
        nf = north_ref[:, at] * jnp.where(row_id == rows - 1, line_of(mask_ref.at[3], c), here)
        sf = jnp.where(row_id == 0, 0.0, pltpu.roll(nf, 1, 0))
        center = (1.0 - here) + here * storage_ref[:, at] + e + w + nf + sf
        jacobi = 1.0 / center
        f = f_ref[:, at]
        smoothed = jacobi * f
        e_ref[:, at] = e
        w_ref[:, at] = w
        s_ref[:, at] = sf
        n_ref[:, at] = nf
        c_ref[:, at] = center
        j_ref[:, at] = jacobi
        sm_ref[:, at] = smoothed
        return energy + fold(jnp.where(row_id == 0, 0.0, f * smoothed))

    energy_part = lax.fori_loop(0, chunks, coefficients, zero)

    @pl.when(has_up)
    def _():
        sm_up.start()

    @pl.when(has_down)
    def _():
        north_up.wait_recv()

    row8 = lax.broadcasted_iota(jnp.int32, (8, span), 0)

    def first_row_of(c, energy):
        at = cols(c)
        south = jnp.where(row8 == 0, nlo_ref[:, at] * line_of(mask_ref.at[4], c), 0.0)
        s_ref[0:8, at] = s_ref[0:8, at] + south
        center = c_ref[0:8, at] + south
        jacobi = 1.0 / center
        f = f_ref[0:8, at]
        smoothed = jacobi * f
        c_ref[0:8, at] = center
        j_ref[0:8, at] = jacobi
        sm_ref[0:8, at] = smoothed
        return energy + fold(jnp.where(row8 == 0, f * smoothed, 0.0))

    energy_part = lax.fori_loop(0, chunks, first_row_of, energy_part)

    @pl.when(has_down)
    def _():
        sm_down.start()

    def lane_sums(v):
        return jnp.sum(v, axis=0, keepdims=True)

    def dots_rows(a, b):
        r = lax.broadcasted_iota(jnp.int32, (8, LANES), 0)
        return jnp.where(r == 0, lane_sums(a), jnp.where(r == 1, lane_sums(b), 0.0))

    def total(block, row):
        return jnp.sum(block[row : row + 1, :], axis=1, keepdims=True)

    def expand(g):
        c = ct_ref[0] * g[0:1, :]
        for k in range(1, coarse):
            c = c + ct_ref[k] * g[k : k + 1, :]
        gc = jnp.sum(jnp.sum(g * c, axis=0, keepdims=True)[:, :half], axis=1, keepdims=True)
        d = dot(c.T, kron_ref[...])
        d = jnp.where(same_half, d, 0.0)
        spread_ref[...] = pick(own_ref[0], d)

        def edge(modes):
            return functools.reduce(
                lambda a, b: a + b,
                [modes[p] * d[:, p * LANES : (p + 1) * LANES] for p in range(ORDER)],
            )

        edge_ref[0] = pick(own_ref[2], edge(down_modes))
        edge_ref[1] = pick(own_ref[3], edge(up_modes))
        return gc

    def spread(c):
        return functools.reduce(
            lambda a, b: a + b,
            [wide(row_modes[p]) * line_of(spread_ref, c, p * LANES) for p in range(ORDER)],
        )

    def wrap(ref):
        ref[:, 0:LANES] = ref[:, width : width + LANES]
        ref[:, width + LANES : width + 2 * LANES] = ref[:, LANES : 2 * LANES]

    def operate(z_ref, c, low, high):
        at = cols(c)
        window = z_ref[:, cols(c, 0, 2 * LANES)]
        size = span + 2 * LANES
        v = window[:, LANES : LANES + span]
        east_v = pltpu.roll(window, size - 1, 1)[:, LANES : LANES + span]
        west_v = pltpu.roll(window, 1, 1)[:, LANES : LANES + span]
        north_v = jnp.where(row_id == rows - 1, high, pltpu.roll(v, rows - 1, 0))
        south_v = jnp.where(row_id == 0, low, pltpu.roll(v, 1, 0))
        image = (
            c_ref[:, at] * v - e_ref[:, at] * east_v - w_ref[:, at] * west_v
            - n_ref[:, at] * north_v - s_ref[:, at] * south_v
        )
        return v, image

    g = unpacked(wait_all(0))
    coarse_energy = expand(g)

    def precondition0(c, carry):
        z0_ref[:, cols(c, LANES)] = sm_ref[:, cols(c)] + spread(c)
        return carry

    lax.fori_loop(0, chunks, precondition0, 0)
    wrap(z0_ref)

    @pl.when(has_down)
    def _():
        sm_up.wait_recv()

    @pl.when(has_up)
    def _():
        sm_down.wait_recv()

    def image0(c, along):
        at = cols(c)
        low = smlo_ref[:, at] + line_of(edge_ref.at[0], c)
        high = smhi_ref[:, at] + line_of(edge_ref.at[1], c)
        v, image = operate(z0_ref, c, low, high)
        im0_ref[:, at] = image
        q_ref[:, at] = j_ref[:, at] * image
        lift(c, image)
        return along + fold(v * image)

    along_part = lax.fori_loop(0, chunks, image0, zero)

    @pl.when(has_up)
    def _():
        q_up.start()

    @pl.when(has_down)
    def _():
        q_down.start()

    send_ref[1, 0:8] = packed_moments()
    send_ref[1, 8:16] = dots_rows(energy_part, along_part)
    send_all(1)
    drain(0)
    sums = wait_all(1)
    energy = total(sums, 8) + coarse_energy
    alpha = energy / total(sums, 9)
    g = g - alpha * unpacked(sums[0:8])
    coarse_energy = expand(g)

    def precondition1(c, acc):
        at = cols(c)
        smoothed = sm_ref[:, at] - alpha * q_ref[:, at]
        residual = f_ref[:, at] - alpha * im0_ref[:, at]
        f_ref[:, at] = residual
        z1_ref[:, cols(c, LANES)] = smoothed + spread(c)
        return acc + fold(residual * smoothed)

    energy_part = lax.fori_loop(0, chunks, precondition1, zero)
    wrap(z1_ref)

    @pl.when(has_down)
    def _():
        q_up.wait_recv()

    @pl.when(has_up)
    def _():
        q_down.wait_recv()

    def image1(c, along):
        at = cols(c)
        low = smlo_ref[:, at] - alpha * qlo_ref[:, at] + line_of(edge_ref.at[0], c)
        high = smhi_ref[:, at] - alpha * qhi_ref[:, at] + line_of(edge_ref.at[1], c)
        v, image = operate(z1_ref, c, low, high)
        im1_ref[:, at] = image
        return along + fold(v * image)

    along_part = lax.fori_loop(0, chunks, image1, zero)
    send_ref[2, 8:16] = dots_rows(energy_part, along_part)
    send_all(2)
    drain(1)
    sums = wait_all(2)
    energy_next = total(sums, 0) + coarse_energy
    beta = energy_next / energy
    alpha_next = energy_next / (total(sums, 1) - beta * energy_next / alpha)

    def finish(c, carry):
        at = cols(c)
        z0 = z0_ref[:, cols(c, LANES)]
        sol_ref[:, at] = alpha * z0 + alpha_next * (z1_ref[:, cols(c, LANES)] + beta * z0)
        res_ref[:, at] = f_ref[:, at] - alpha_next * (im1_ref[:, at] + beta * im0_ref[:, at])
        return carry

    lax.fori_loop(0, chunks, finish, 0)

    @pl.when(has_up)
    def _():
        north_up.wait_send()
        sm_up.wait_send()
        q_up.wait_send()

    @pl.when(has_down)
    def _():
        sm_down.wait_send()
        q_down.wait_send()

    drain(2)


def body(forcing, east, north, storage, coarse_inverse, membership, land):
    n = lax.axis_size("gy")
    rows, width = forcing.shape
    basins, coarse, _ = coarse_inverse.shape
    inverse = jnp.transpose(coarse_inverse, (1, 2, 0))
    by_row, kron = tables()
    field = pltpu.VMEM((rows, width), jnp.float32)
    padded = pltpu.VMEM((rows, width + 2 * LANES), jnp.float32)
    line = pltpu.VMEM((1, width), jnp.float32)
    blocks = width // LANES
    hbm = pl.BlockSpec(memory_space=pltpu.HBM)
    vmem = pl.BlockSpec(memory_space=pltpu.VMEM)
    return pl.pallas_call(
        functools.partial(kernel, n),
        out_shape=[jax.ShapeDtypeStruct((rows, width), jnp.float32)] * 2,
        in_specs=[hbm] * 9,
        out_specs=[vmem] * 2,
        scratch_shapes=[
            pltpu.VMEM((coarse, coarse, basins), jnp.float32),
            pltpu.VMEM(membership.shape, jnp.int32),
            pltpu.VMEM(land.shape, jnp.int32),
            pltpu.VMEM(by_row.shape, jnp.float32),
            pltpu.VMEM(kron.shape, jnp.float32),
            field, padded, field, field,
            field, field, field, field, field, field, field, padded, padded, field, field, field,
            pltpu.VMEM((5, blocks, LANES), jnp.float32),
            pltpu.VMEM((4, blocks, LANES), jnp.float32),
            pltpu.VMEM((blocks, ORDER * LANES), jnp.float32),
            pltpu.VMEM((2, blocks, LANES), jnp.float32),
            pltpu.VMEM((blocks, ORDER * LANES), jnp.float32),
            pltpu.VMEM((coarse, coarse, LANES), jnp.float32),
            line, line, line, line, line,
            pltpu.VMEM((3, 16, LANES), jnp.float32),
            pltpu.VMEM((3, n, 16, LANES), jnp.float32),
            pltpu.SemaphoreType.DMA((10,)),
            pltpu.SemaphoreType.DMA((5,)),
            pltpu.SemaphoreType.DMA((5,)),
            pltpu.SemaphoreType.DMA((3, n)),
            pltpu.SemaphoreType.DMA((3, n)),
        ],
        compiler_params=pltpu.CompilerParams(
            collective_id=0, has_side_effects=True, vmem_limit_bytes=48 * 1024 * 1024
        ),
        name="solve",
    )(*(
        pltpu.with_memory_space_constraint(x, pltpu.HBM)
        for x in (
            forcing, east, north, storage, inverse, membership, land,
            jnp.asarray(by_row), jnp.asarray(kron),
        )
    ))


def solution(mesh):
    return jax.shard_map(
        body,
        mesh=mesh,
        in_specs=(
            P(("ens", "gy"), None),
            P("gy", None),
            P("gy", None),
            P("gy", None),
            P(),
            P(),
            P(),
        ),
        out_specs=(P(("ens", "gy"), None), P(("ens", "gy"), None)),
        check_vma=False,
    )
```

```python
import functools

import jax
import jax.numpy as jnp
import numpy as np
from jax import lax
from jax.experimental import pallas as pl
from jax.experimental.pallas import tpu as pltpu
from jax.sharding import PartitionSpec as P

TILE = 64
ORDER = 4
LANES = 128
BLOCKS = 8
MESH = pl.DeviceIdType.MESH


def tables():
    degree = np.arange(ORDER, dtype=np.float64)
    local = np.arange(TILE, dtype=np.float64)
    modes = np.cos(np.pi * degree[:, None] * (local[None, :] + 0.5) / TILE).astype(np.float32)
    by_row = np.repeat(modes[:, :, None], LANES, axis=2)
    kron = np.zeros((ORDER * ORDER, ORDER * LANES), np.float32)
    for p in range(ORDER):
        for q in range(ORDER):
            kron[p * ORDER + q, p * LANES : (p + 1) * LANES] = np.tile(modes[q], LANES // TILE)
    return by_row, kron


def halves(x):
    high = x.astype(jnp.bfloat16)
    return high, (x - high.astype(jnp.float32)).astype(jnp.bfloat16)


def one_pass(a, b, contract):
    return lax.dot_general(a, b, (contract, ((), ())), preferred_element_type=jnp.float32)


def pick(a, b):
    high, low = halves(b)
    a = a.astype(jnp.bfloat16)
    return one_pass(a, high, ((1,), (0,))) + one_pass(a, low, ((1,), (0,)))


def dot(a, b, contract=((1,), (0,))):
    (ah, al), (bh, bl) = halves(a), halves(b)
    return one_pass(ah, bh, contract) + (one_pass(ah, bl, contract) + one_pass(al, bh, contract))


def kernel(
    n,
    forcing_hbm, east_hbm, north_hbm, storage_hbm, inv_hbm,
    membership_hbm, land_hbm, by_row_hbm, kron_hbm,
    sol_ref, res_ref,
    inv_ref, membership_ref, land_ref, by_row_ref, kron_ref,
    f_ref, east_ref, north_ref, storage_ref,
    e_ref, w_ref, s_ref, c_ref, j_ref, sm_ref, q_ref, z0_ref, z1_ref, im0_ref, im1_ref, n_ref,
    mask_ref, own_ref, spread_ref, edge_ref, lift_ref, ct_ref,
    nlo_ref, smlo_ref, smhi_ref, qlo_ref, qhi_ref,
    send_ref, recv_ref,
    in_sem, row_send_sem, row_recv_sem, all_send_sem, all_recv_sem,
):
    rows, width = f_ref.shape
    coarse = inv_ref.shape[0]
    blocks = width // LANES
    half = LANES // 2
    span = BLOCKS * LANES
    chunks = width // span
    tile_rows = membership_ref.shape[0]
    me = lax.axis_index("gy")
    start = me * rows
    has_up = me < n - 1
    has_down = me > 0

    def load(src, dst, k):
        return pltpu.make_async_copy(src, dst, in_sem.at[k])

    tables_in = [
        load(membership_hbm, membership_ref, 5),
        load(land_hbm, land_ref, 6),
        load(by_row_hbm, by_row_ref, 7),
        load(kron_hbm, kron_ref, 8),
        load(inv_hbm, inv_ref, 9),
    ]
    loads = [
        load(forcing_hbm, f_ref, 0),
        load(north_hbm, north_ref, 1),
        load(east_hbm, east_ref.at[:, pl.ds(LANES, width)], 2),
        load(east_hbm.at[:, pl.ds(width - LANES, LANES)], east_ref.at[:, pl.ds(0, LANES)], 3),
        load(storage_hbm, storage_ref, 4),
    ]
    for copy in tables_in + loads:
        copy.start()

    barrier = pltpu.get_barrier_semaphore()

    def greet(k, carry):
        pl.semaphore_signal(
            barrier, inc=1, device_id={"gy": lax.rem(me + k, n)}, device_id_type=MESH
        )
        return carry

    lax.fori_loop(1, n, greet, 0, unroll=n <= 16)

    for copy in tables_in:
        copy.wait()

    own_row = start // TILE
    up_row = jnp.minimum((start + rows) // TILE, tile_rows - 1)
    down_row = jnp.maximum(start - 1, 0) // TILE
    local_own = pl.multiple_of(lax.rem(start, TILE), rows)
    local_up = lax.rem(start + rows, TILE)
    local_down = lax.rem(start + TILE - 1, TILE)

    tiles = membership_ref.shape[1]
    tile_id = lax.broadcasted_iota(jnp.int32, (blocks, tiles), 1)
    block_id = lax.broadcasted_iota(jnp.int32, (blocks, tiles), 0)
    even = tile_id == 2 * block_id
    odd = tile_id == 2 * block_id + 1
    lane = lax.broadcasted_iota(jnp.int32, (blocks, LANES), 1)
    left = lane < half
    basin_of_lane = jnp.where(left, lane, lane - half)

    def columns(table, row):
        line = table[pl.ds(row, 1), :].astype(jnp.float32)
        first = jnp.sum(jnp.where(even, line, 0.0), axis=1, keepdims=True)
        second = jnp.sum(jnp.where(odd, line, 0.0), axis=1, keepdims=True)
        return (
            jnp.broadcast_to(first, (blocks, LANES)),
            jnp.broadcast_to(second, (blocks, LANES)),
        )

    def owned(row, wet0, wet1):
        first, second = columns(membership_ref, row)
        which = jnp.where(left, first, second)
        hit = which == basin_of_lane.astype(jnp.float32)
        return jnp.where(hit, jnp.where(left, wet0, wet1), 0.0)

    def wets(row):
        first, second = columns(land_ref, row)
        return 1.0 - first, 1.0 - second

    wet0, wet1 = wets(own_row)
    wet = jnp.where(left, wet0, wet1)
    own_ref[0] = owned(own_row, wet0, wet1)
    own_ref[1] = own_ref[0].T
    row_modes = [by_row_ref[p, pl.ds(local_own, rows), :] for p in range(ORDER)]
    up_modes = [by_row_ref[p, pl.ds(local_up, 1), :] for p in range(ORDER)]
    down_modes = [by_row_ref[p, pl.ds(local_down, 1), :] for p in range(ORDER)]

    def wide(v):
        return jnp.concatenate([v] * BLOCKS, axis=1)

    def group(c):
        return pl.ds(pl.multiple_of(c * BLOCKS, BLOCKS), BLOCKS)

    def line_of(ref, c, lane0=0):
        block = ref[group(c), lane0 : lane0 + LANES]
        return jnp.concatenate([block[t : t + 1, :] for t in range(BLOCKS)], axis=1)

    def cols(c, offset=0, extra=0):
        return pl.ds(pl.multiple_of(c * span + offset, LANES), span + extra)

    row_id = lax.broadcasted_iota(jnp.int32, (rows, span), 0)

    sub = lax.broadcasted_iota(jnp.int32, (8, LANES), 0)

    def sum_rows(parts):
        for bit in (4, 2, 1):
            lower = lax.rem(sub // bit, 2) == 0
            merged = []
            for t in range(bit):
                a, b = parts[t], parts[t + bit]
                other = jnp.where(lower, b, a)
                turned = pltpu.roll(other, 8 - bit, 0)
                if bit != 4:
                    turned = jnp.where(lower, turned, pltpu.roll(other, bit, 0))
                merged.append(jnp.where(lower, a, b) + turned)
            parts = merged
        return parts[0]

    def lift(c, field):
        for p in range(ORDER):
            parts = []
            for t in range(BLOCKS):
                block = field[:, t * LANES : (t + 1) * LANES] * row_modes[p]
                parts.append(functools.reduce(
                    lambda a, b: a + b, [block[i : i + 8] for i in range(0, rows, 8)]
                ))
            lift_ref[group(c), p * LANES : (p + 1) * LANES] = sum_rows(parts)

    half_row = lax.broadcasted_iota(jnp.int32, (LANES, ORDER * LANES), 0) < half
    half_col = (
        lax.rem(lax.broadcasted_iota(jnp.int32, (LANES, ORDER * LANES), 1), LANES) < half
    )
    same_half = half_row == half_col
    left8 = lax.broadcasted_iota(jnp.int32, (coarse // 2, LANES), 1) < half

    def packed_moments():
        sums = pick(own_ref[1], lift_ref[...])
        sums = jnp.where(same_half, sums, 0.0)
        g = dot(kron_ref[...], sums, ((1,), (1,)))
        g = g + pltpu.roll(g, half, 1)
        return jnp.where(left8, g[: coarse // 2], g[coarse // 2 :])

    def unpacked(packed):
        turned = pltpu.roll(packed, half, 1)
        return jnp.concatenate(
            [jnp.where(left8, packed, turned), jnp.where(left8, turned, packed)], axis=0
        )

    def remote(src, dst, send_sem, recv_sem, peer):
        return pltpu.make_async_remote_copy(
            src_ref=src, dst_ref=dst, send_sem=send_sem, recv_sem=recv_sem,
            device_id={"gy": peer}, device_id_type=MESH,
        )

    part = (8, 10, 2)
    first_row = (0, 0, 8)

    def exchange(k, peer_step):
        peer = lax.rem(me + peer_step, n)
        window = pl.ds(first_row[k], part[k])
        return remote(
            send_ref.at[k, window], recv_ref.at[k, me, window],
            all_send_sem.at[k, peer_step], all_recv_sem.at[k, me], peer,
        )

    def send_all(k):
        def go(i, carry):
            step = n // 2 + (2 * (i % 2) - 1) * ((i + 1) // 2)
            exchange(k, step).start()
            return carry

        if n <= 16:
            for i in range(n - 1):
                go(i, 0)
        else:
            lax.fori_loop(0, n - 1, go, 0)
        window = pl.ds(first_row[k], part[k])
        recv_ref[k, me, window] = send_ref[k, window]

    def wait_all(k):
        window = pl.ds(first_row[k], part[k])

        def go(step, carry):
            peer = lax.rem(me + step, n)
            remote(
                send_ref.at[k, window], recv_ref.at[k, peer, window],
                all_send_sem.at[k, step], all_recv_sem.at[k, peer], peer,
            ).wait_recv()
            return carry

        lax.fori_loop(1, n, go, 0, unroll=n <= 16)
        parts = [recv_ref[k, i, first_row[k] : first_row[k] + part[k], :] for i in range(n)]
        while len(parts) > 1:
            parts = [parts[i] + parts[i + 1] for i in range(0, len(parts) - 1, 2)] + (
                [parts[-1]] if len(parts) % 2 else []
            )
        return parts[0]

    def drain(k):
        def go(step, carry):
            exchange(k, step).wait_send()
            return carry

        lax.fori_loop(1, n, go, 0, unroll=n <= 16)

    def row_up(src, dst, k):
        return remote(src, dst, row_send_sem.at[k], row_recv_sem.at[k], me + 1)

    def row_down(src, dst, k):
        return remote(src, dst, row_send_sem.at[k], row_recv_sem.at[k], me - 1)

    last = pl.ds(rows - 1, 1)
    first = pl.ds(0, 1)
    north_up = row_up(north_ref.at[last], nlo_ref, 0)
    sm_up = row_up(sm_ref.at[last], smlo_ref, 1)
    sm_down = row_down(sm_ref.at[first], smhi_ref, 2)
    q_up = row_up(q_ref.at[last], qlo_ref, 3)
    q_down = row_down(q_ref.at[first], qhi_ref, 4)

    @pl.when(jnp.logical_not(has_down))
    def _():
        for ref in (nlo_ref, smlo_ref, qlo_ref):
            ref[...] = jnp.zeros_like(ref)

    @pl.when(jnp.logical_not(has_up))
    def _():
        for ref in (smhi_ref, qhi_ref):
            ref[...] = jnp.zeros_like(ref)

    loads[0].wait()

    def first_moments(c, carry):
        lift(c, f_ref[:, cols(c)])
        return carry

    lax.fori_loop(0, chunks, first_moments, 0)
    send_ref[0, 0:8] = packed_moments()
    loads[1].wait()
    pl.semaphore_wait(barrier, n - 1)

    @pl.when(has_up)
    def _():
        north_up.start()

    send_all(0)

    east_wet = jnp.where(
        lane == half - 1, wet1, jnp.where(lane == LANES - 1, pltpu.roll(wet0, blocks - 1, 0), wet)
    )
    west_wet = jnp.where(lane == 0, pltpu.roll(wet1, 1, 0), jnp.where(lane == half, wet0, wet))
    up0, up1 = wets(up_row)
    down0, down1 = wets(down_row)
    mask_ref[0] = wet
    mask_ref[1] = wet * east_wet
    mask_ref[2] = wet * west_wet
    mask_ref[3] = jnp.where(has_up, wet * jnp.where(left, up0, up1), 0.0)
    mask_ref[4] = jnp.where(has_down, wet * jnp.where(left, down0, down1), 0.0)
    own_ref[2] = owned(down_row, down0, down1)
    own_ref[3] = owned(up_row, up0, up1)

    loads[2].wait()
    loads[3].wait()
    loads[4].wait()

    for k in range(coarse):
        ct_ref[k] = jnp.concatenate([inv_ref[k]] * 2, axis=1)


    zero = jnp.zeros((8, LANES), jnp.float32)

    def fold(v):
        parts = [
            v[i : i + 8, t * LANES : (t + 1) * LANES]
            for i in range(0, v.shape[0], 8)
            for t in range(BLOCKS)
        ]
        while len(parts) > 1:
            parts = [parts[i] + parts[i + 1] for i in range(0, len(parts), 2)]
        return parts[0]

    def coefficients(c, energy):
        at = cols(c)
        here = line_of(mask_ref.at[0], c)
        raw = east_ref[:, pl.ds(pl.multiple_of(c * span, LANES), span + LANES)]
        e = raw[:, LANES:] * line_of(mask_ref.at[1], c)
        w = pltpu.roll(raw, 1, 1)[:, LANES:] * line_of(mask_ref.at[2], c)
        nf = north_ref[:, at] * jnp.where(row_id == rows - 1, line_of(mask_ref.at[3], c), here)
        sf = jnp.where(row_id == 0, 0.0, pltpu.roll(nf, 1, 0))
        center = (1.0 - here) + here * storage_ref[:, at] + e + w + nf + sf
        jacobi = 1.0 / center
        f = f_ref[:, at]
        smoothed = jacobi * f
        e_ref[:, at] = e
        w_ref[:, at] = w
        s_ref[:, at] = sf
        n_ref[:, at] = nf
        c_ref[:, at] = center
        j_ref[:, at] = jacobi
        sm_ref[:, at] = smoothed
        return energy + fold(jnp.where(row_id == 0, 0.0, f * smoothed))

    energy_part = lax.fori_loop(0, chunks, coefficients, zero)

    @pl.when(has_up)
    def _():
        sm_up.start()

    @pl.when(has_down)
    def _():
        north_up.wait_recv()

    row8 = lax.broadcasted_iota(jnp.int32, (8, span), 0)

    def first_row_of(c, energy):
        at = cols(c)
        south = jnp.where(row8 == 0, nlo_ref[:, at] * line_of(mask_ref.at[4], c), 0.0)
        s_ref[0:8, at] = s_ref[0:8, at] + south
        center = c_ref[0:8, at] + south
        jacobi = 1.0 / center
        f = f_ref[0:8, at]
        smoothed = jacobi * f
        c_ref[0:8, at] = center
        j_ref[0:8, at] = jacobi
        sm_ref[0:8, at] = smoothed
        return energy + fold(jnp.where(row8 == 0, f * smoothed, 0.0))

    energy_part = lax.fori_loop(0, chunks, first_row_of, energy_part)

    @pl.when(has_down)
    def _():
        sm_down.start()

    def lane_sums(v):
        return jnp.sum(v, axis=0, keepdims=True)

    def dots_rows(a, b):
        r = lax.broadcasted_iota(jnp.int32, (8, LANES), 0)
        return jnp.where(r == 0, lane_sums(a), jnp.where(r == 1, lane_sums(b), 0.0))

    def total(block, row):
        return jnp.sum(block[row : row + 1, :], axis=1, keepdims=True)

    def expand(g):
        c = ct_ref[0] * g[0:1, :]
        for k in range(1, coarse):
            c = c + ct_ref[k] * g[k : k + 1, :]
        gc = jnp.sum(jnp.sum(g * c, axis=0, keepdims=True)[:, :half], axis=1, keepdims=True)
        d = dot(c.T, kron_ref[...])
        d = jnp.where(same_half, d, 0.0)
        spread_ref[...] = pick(own_ref[0], d)

        def edge(modes):
            return functools.reduce(
                lambda a, b: a + b,
                [modes[p] * d[:, p * LANES : (p + 1) * LANES] for p in range(ORDER)],
            )

        edge_ref[0] = pick(own_ref[2], edge(down_modes))
        edge_ref[1] = pick(own_ref[3], edge(up_modes))
        return gc

    def spread(c):
        return functools.reduce(
            lambda a, b: a + b,
            [wide(row_modes[p]) * line_of(spread_ref, c, p * LANES) for p in range(ORDER)],
        )

    def wrap(ref):
        ref[:, 0:LANES] = ref[:, width : width + LANES]
        ref[:, width + LANES : width + 2 * LANES] = ref[:, LANES : 2 * LANES]

    def operate(z_ref, c, low, high):
        at = cols(c)
        window = z_ref[:, cols(c, 0, 2 * LANES)]
        size = span + 2 * LANES
        v = window[:, LANES : LANES + span]
        east_v = pltpu.roll(window, size - 1, 1)[:, LANES : LANES + span]
        west_v = pltpu.roll(window, 1, 1)[:, LANES : LANES + span]
        north_v = jnp.where(row_id == rows - 1, high, pltpu.roll(v, rows - 1, 0))
        south_v = jnp.where(row_id == 0, low, pltpu.roll(v, 1, 0))
        image = (
            c_ref[:, at] * v - e_ref[:, at] * east_v - w_ref[:, at] * west_v
            - n_ref[:, at] * north_v - s_ref[:, at] * south_v
        )
        return v, image

    g = unpacked(wait_all(0))
    coarse_energy = expand(g)

    def precondition0(c, carry):
        z0_ref[:, cols(c, LANES)] = sm_ref[:, cols(c)] + spread(c)
        return carry

    lax.fori_loop(0, chunks, precondition0, 0)
    wrap(z0_ref)

    @pl.when(has_down)
    def _():
        sm_up.wait_recv()

    @pl.when(has_up)
    def _():
        sm_down.wait_recv()

    def image0(c, along):
        at = cols(c)
        low = smlo_ref[:, at] + line_of(edge_ref.at[0], c)
        high = smhi_ref[:, at] + line_of(edge_ref.at[1], c)
        v, image = operate(z0_ref, c, low, high)
        im0_ref[:, at] = image
        q_ref[:, at] = j_ref[:, at] * image
        lift(c, image)
        return along + fold(v * image)

    along_part = lax.fori_loop(0, chunks, image0, zero)

    @pl.when(has_up)
    def _():
        q_up.start()

    @pl.when(has_down)
    def _():
        q_down.start()

    send_ref[1, 0:8] = packed_moments()
    send_ref[1, 8:16] = dots_rows(energy_part, along_part)
    send_all(1)
    drain(0)
    sums = wait_all(1)
    energy = total(sums, 8) + coarse_energy
    alpha = energy / total(sums, 9)
    g = g - alpha * unpacked(sums[0:8])
    coarse_energy = expand(g)

    def precondition1(c, acc):
        at = cols(c)
        smoothed = sm_ref[:, at] - alpha * q_ref[:, at]
        residual = f_ref[:, at] - alpha * im0_ref[:, at]
        f_ref[:, at] = residual
        z1_ref[:, cols(c, LANES)] = smoothed + spread(c)
        return acc + fold(residual * smoothed)

    energy_part = lax.fori_loop(0, chunks, precondition1, zero)
    wrap(z1_ref)

    @pl.when(has_down)
    def _():
        q_up.wait_recv()

    @pl.when(has_up)
    def _():
        q_down.wait_recv()

    def image1(c, along):
        at = cols(c)
        low = smlo_ref[:, at] - alpha * qlo_ref[:, at] + line_of(edge_ref.at[0], c)
        high = smhi_ref[:, at] - alpha * qhi_ref[:, at] + line_of(edge_ref.at[1], c)
        v, image = operate(z1_ref, c, low, high)
        im1_ref[:, at] = image
        return along + fold(v * image)

    along_part = lax.fori_loop(0, chunks, image1, zero)
    send_ref[2, 8:16] = dots_rows(energy_part, along_part)
    send_all(2)
    drain(1)
    @pl.when(has_up)
    def _():
        north_up.wait_send()
        sm_up.wait_send()
        q_up.wait_send()

    @pl.when(has_down)
    def _():
        sm_down.wait_send()
        q_down.wait_send()

    drain(2)
    sums = wait_all(2)
    energy_next = total(sums, 0) + coarse_energy
    beta = energy_next / energy
    alpha_next = energy_next / (total(sums, 1) - beta * energy_next / alpha)

    def finish(c, carry):
        at = cols(c)
        z0 = z0_ref[:, cols(c, LANES)]
        sol_ref[:, at] = alpha * z0 + alpha_next * (z1_ref[:, cols(c, LANES)] + beta * z0)
        res_ref[:, at] = f_ref[:, at] - alpha_next * (im1_ref[:, at] + beta * im0_ref[:, at])
        return carry

    lax.fori_loop(0, chunks, finish, 0)


def body(forcing, east, north, storage, coarse_inverse, membership, land):
    n = lax.axis_size("gy")
    rows, width = forcing.shape
    basins, coarse, _ = coarse_inverse.shape
    inverse = jnp.transpose(coarse_inverse, (1, 2, 0))
    by_row, kron = tables()
    field = pltpu.VMEM((rows, width), jnp.float32)
    padded = pltpu.VMEM((rows, width + 2 * LANES), jnp.float32)
    line = pltpu.VMEM((1, width), jnp.float32)
    blocks = width // LANES
    hbm = pl.BlockSpec(memory_space=pltpu.HBM)
    vmem = pl.BlockSpec(memory_space=pltpu.VMEM)
    return pl.pallas_call(
        functools.partial(kernel, n),
        out_shape=[jax.ShapeDtypeStruct((rows, width), jnp.float32)] * 2,
        in_specs=[hbm] * 9,
        out_specs=[vmem] * 2,
        scratch_shapes=[
            pltpu.VMEM((coarse, coarse, basins), jnp.float32),
            pltpu.VMEM(membership.shape, jnp.int32),
            pltpu.VMEM(land.shape, jnp.int32),
            pltpu.VMEM(by_row.shape, jnp.float32),
            pltpu.VMEM(kron.shape, jnp.float32),
            field, padded, field, field,
            field, field, field, field, field, field, field, padded, padded, field, field, field,
            pltpu.VMEM((5, blocks, LANES), jnp.float32),
            pltpu.VMEM((4, blocks, LANES), jnp.float32),
            pltpu.VMEM((blocks, ORDER * LANES), jnp.float32),
            pltpu.VMEM((2, blocks, LANES), jnp.float32),
            pltpu.VMEM((blocks, ORDER * LANES), jnp.float32),
            pltpu.VMEM((coarse, coarse, LANES), jnp.float32),
            line, line, line, line, line,
            pltpu.VMEM((3, 16, LANES), jnp.float32),
            pltpu.VMEM((3, n, 16, LANES), jnp.float32),
            pltpu.SemaphoreType.DMA((10,)),
            pltpu.SemaphoreType.DMA((5,)),
            pltpu.SemaphoreType.DMA((5,)),
            pltpu.SemaphoreType.DMA((3, n)),
            pltpu.SemaphoreType.DMA((3, n)),
        ],
        compiler_params=pltpu.CompilerParams(
            collective_id=0, has_side_effects=True, vmem_limit_bytes=48 * 1024 * 1024
        ),
        name="solve",
    )(*(
        pltpu.with_memory_space_constraint(x, pltpu.HBM)
        for x in (
            forcing, east, north, storage, inverse, membership, land,
            jnp.asarray(by_row), jnp.asarray(kron),
        )
    ))


def solution(mesh):
    return jax.shard_map(
        body,
        mesh=mesh,
        in_specs=(
            P(("ens", "gy"), None),
            P("gy", None),
            P("gy", None),
            P("gy", None),
            P(),
            P(),
            P(),
        ),
        out_specs=(P(("ens", "gy"), None), P(("ens", "gy"), None)),
        check_vma=False,
    )
```
